128 devices in a mesh: blk: 16 (over x, z), expert: 8 (over y, core).
Axes of the slice: x: 4, y: 4, z: 4, core: 2. Of those that a mesh axis runs over, the one named last changes fastest.
Arguments:
- hidden: bfloat16 [16, 32, 2, 2304], P('blk', 'expert'), may hold values from -6 to 6
- query: bfloat16 [16, 32, 2, 2304], P('blk', 'expert'), may hold values from -8 to 8
- new_key: bfloat16 [16, 32, 2, 2304], P('blk', 'expert'), may hold values from -8 to 8
- new_value: bfloat16 [16, 32, 2, 2304], P('blk', 'expert'), may hold values from -18 to 18
- prompt_key: bfloat16 [32, 1024, 2304], P('expert', 'blk'), may hold values from -8 to 8
- prompt_value: bfloat16 [32, 1024, 2304], P('expert', 'blk'), may hold values from -18 to 18
- prompt_len: int32 [32], replicated, may hold values from 128 to 1024, as said below
- live_blocks: int32 [32, 64], replicated, may hold values from 0 to 1
- tail_key: bfloat16 [16, 32, 64, 2304], P('blk', 'expert'), may hold values from -8 to 8
- tail_value: bfloat16 [16, 32, 64, 2304], P('blk', 'expert'), may hold values from -18 to 18
- tail_len: int32 [16, 32], replicated, may hold values from 1 to 64, as said below
- tail_source: int32 [16, 32], replicated, may hold values from 0 to 15, as said below
- routes: int32 [16, 32, 2, 2], P('blk', 'expert'), may hold values from 0 to 7, all different within a row; in each aligned block of 8 rows (0 to 7, 8 to 15, ..., all dimensions but the last counted through in order) at most 4 rows name the same one
- router: float32 [2304, 8], replicated, may hold values from -0.125 to 0.125
- ffn_gain: float32 [2304], replicated, may hold values from 0.25 to 1.75
- w_gate: bfloat16 [8, 2304, 5760], P('expert', None, 'blk'), may hold values from -0.125 to 0.125
- w_up: bfloat16 [8, 2304, 5760], P('expert', None, 'blk'), may hold values from -0.125 to 0.125
- w_down: bfloat16 [8, 5760, 2304], P('expert', 'blk'), may hold values from -0.078125 to 0.078125
- score_weight: float32 [2304], replicated, may hold values from -0.125 to 0.125
Outputs:
- layer_out: bfloat16 [16, 32, 2, 2304], P('blk', 'expert')
- score: float32 [16, 32, 2], P('blk', 'expert')
The draws below stay inside these ranges and needn't reach their ends.
Inputs may be any that keep to these rules, and one draw needn't show every extreme that they name: `prompt_len`: some prompt has all 1024 positions cached. `tail_len`: some sample has a tail of exactly 64 positions. For each prompt p, tail_source[:, p] is a permutation of the 16 samples; half of the slots hold another sample's tail. `routes`: in the rows of one device (aligned blocks of 8 rows in the order of the leading dimensions) each row names 2 different experts and no expert is named by more than 4 rows; some expert is named by exactly 4 rows.
All inputs are finite; a program needn't handle non-finite values.
Results may differ from the reference program's by a relative error of at most 0.025.
Values may be sent and summed in bfloat16 or wider, within the bound.
No kernel may reach another device: no remote copies, remote signals or barrier semaphores. Data moves between devices by JAX's collectives and lax.ppermute only.
A program may use at most 256 MiB of HBM per device.

```python
import math
import jax
import jax.numpy as jnp
import numpy as np
from jax import lax

D = 2304
HEADS = 36
HDIM = 64
FF = 5760
EXPERTS = 8
TOP = 2
NEW = 2
KVB = 16
PR_DEV = 4
TAIL = 64
SAMPLES = 16
PROMPTS = 32
CTX = 1024
BLOCKS = 64
CAP = 4


def prompt_lengths(key):
    lengths = jax.random.randint(jax.random.fold_in(key, 11), (PROMPTS,), CTX // 8, CTX + 1)
    fullest = jax.random.randint(jax.random.fold_in(key, 12), (), 0, PROMPTS)
    return lengths.at[fullest].set(CTX).astype(jnp.int32)


def live_table(key):
    return (jax.random.randint(jax.random.fold_in(key, 41), (PROMPTS, BLOCKS), 0, 4) > 0).astype(jnp.int32)


def owner_column(column_key):
    order = jax.random.permutation(column_key, SAMPLES)
    moved = order[:SAMPLES // 2]
    return jnp.arange(SAMPLES).at[moved].set(jnp.roll(moved, -1))


def tail_owners(key):
    column_keys = jax.random.split(jax.random.fold_in(key, 31), PROMPTS)
    columns = jax.vmap(owner_column)(column_keys)
    return columns.T.astype(jnp.int32)


def draw_query(key, part):
    noise_key = jax.random.fold_in(key, 1)
    values = jnp.clip(jax.random.normal(noise_key, (SAMPLES, PROMPTS, NEW, D), jnp.float32) * 1.5, -8.0, 8.0)
    return values.astype(jnp.bfloat16)


def draw_new_key(key, part):
    noise_key = jax.random.fold_in(key, 2)
    values = jnp.clip(jax.random.normal(noise_key, (SAMPLES, PROMPTS, NEW, D), jnp.float32), -6.0, 6.0)
    return values.astype(jnp.bfloat16)


def draw_prompt_key(key, part):
    noise_key = jax.random.fold_in(key, 3)
    values = jnp.clip(jax.random.normal(noise_key, (PROMPTS, CTX, D), jnp.float32), -6.0, 6.0)
    return values.astype(jnp.bfloat16)


def draw_tail_key(key, part):
    noise_key = jax.random.fold_in(key, 4)
    values = jnp.clip(jax.random.normal(noise_key, (SAMPLES, PROMPTS, TAIL, D), jnp.float32), -6.0, 6.0)
    return values.astype(jnp.bfloat16)


def draw_prompt_len(key, part):
    return prompt_lengths(key)


def draw_live_blocks(key, part):
    return live_table(key)


def draw_tail_len(key, part):
    lengths = jax.random.randint(jax.random.fold_in(key, 21), (SAMPLES, PROMPTS), 1, TAIL + 1)
    row_pick = jax.random.randint(jax.random.fold_in(key, 22), (), 0, SAMPLES)
    col_pick = jax.random.randint(jax.random.fold_in(key, 23), (), 0, PROMPTS)
    return lengths.at[row_pick, col_pick].set(TAIL).astype(jnp.int32)


def draw_tail_source(key, part):
    return tail_owners(key)


def block_levels(rng, shape, pieces, least, largest):
    factor_of = 1.0
    for position, shards_of in pieces:
        draws = jax.random.uniform(jax.random.fold_in(jax.random.fold_in(rng, 6), position), (shards_of,), jnp.float32, least / len(pieces), largest / len(pieces))
        factor_of = factor_of * jnp.repeat(jnp.exp(draws), shape[position] // shards_of).reshape((-1,) + (1,) * (len(shape) - 1 - position))
    return factor_of


def assign_block(key, own, number, rows, amount, top, reach, lean):
    sequence = jax.random.permutation(key, amount)
    packed, ordinary = load_shares(amount, rows * top, reach, lean, True), load_shares(amount, rows * top, reach, lean, False)
    places = jnp.arange(amount)

    def named(sizes, turn):
        used = int((sizes > 0).sum())
        fixed = max(1, used // 4)
        shifted = fixed + (places - fixed + turn * (used - fixed)) % max(1, amount - fixed)
        return jnp.zeros((amount,), jnp.int32).at[sequence[jnp.where(places < fixed, places, shifted)]].set(jnp.asarray(sizes, jnp.int32))

    sizes = jnp.where(number % 4 == 0, named(packed, number // 4), named(ordinary, number - number // 4 - 1))
    mixed = jax.random.permutation(jax.random.fold_in(own, 3), amount)
    giver, receiver = mixed[0:amount // 2 * 2:2], mixed[1:amount // 2 * 2:2]
    slack = jnp.minimum(sizes[giver] - 1, reach - sizes[receiver]) // 2
    slack = jnp.where((giver == sequence[0]) | (receiver == sequence[0]) | (sizes[receiver] == 0), 0, jnp.maximum(slack, 0))
    shifted = jax.random.randint(jax.random.fold_in(own, 4), (amount // 2,), 0, 1 << 20) % (slack + 1)
    sizes = sizes.at[giver].add(-shifted).at[receiver].add(shifted)
    items = jnp.searchsorted(jnp.cumsum(sizes), jnp.arange(rows * top), side="right").astype(jnp.int32)
    table = items.reshape(top, rows).T
    table = table[jax.random.permutation(jax.random.fold_in(own, 1), rows)]
    turn = jax.random.randint(jax.random.fold_in(own, 2), (rows, 1), 0, top)
    return jnp.take_along_axis(table, (jnp.arange(top)[None, :] + turn) % top, axis=1)


def load_shares(number_of, total, bound, lean, full):
    loads = [(1 << 20) // math.isqrt(grade ** lean) + 1 for grade in range(1, number_of + 1)]
    largest = bound if full else min(bound, max(-(-total // number_of), total * loads[0] // sum(loads)))
    least = 1 if total - largest >= number_of - 1 else 0
    holding, rest = [largest] + [least] * (number_of - 1), total - largest - least * (number_of - 1)
    while rest > 0:
        movable = [i for i in range(1, number_of) if holding[i] < largest] or [i for i in range(1, number_of) if holding[i] < bound]
        pool, budget = sum([loads[i] for i in movable]), rest
        for i in movable:
            more = min(bound - holding[i], max(1, budget * loads[i] // pool), rest)
            holding[i] = holding[i] + more
            rest = rest - more
    return np.array(holding)


def gaussian(rng, dims, spread, most, cuts=(), dtype=jnp.bfloat16):
    array = jax.random.normal(rng, dims, jnp.float32) * spread
    if len(cuts) > 0:
        array = block_levels(rng, dims, cuts, -0.22, 0.18) * array
    return jnp.clip(array, min=-most, max=most).astype(dtype)


def setup_inputs(seed: int = 0) -> dict:
    seeds = jax.random.split(jax.random.key(seed), 20)
    hidden = gaussian(seeds[0], (SAMPLES, PROMPTS, NEW, D), 1.0, 6.0, ((0, 16), (1, 8)))
    query = draw_query(jax.random.fold_in(seeds[19], 71), 0)
    new_key = draw_new_key(jax.random.fold_in(seeds[19], 71), 0)
    new_value = gaussian(seeds[3], (SAMPLES, PROMPTS, NEW, D), 3.0, 18.0, ((0, 16), (1, 8)))
    prompt_key = draw_prompt_key(jax.random.fold_in(seeds[19], 71), 0)
    prompt_value = gaussian(seeds[5], (PROMPTS, CTX, D), 3.0, 18.0, ((0, 8), (1, 16)))
    prompt_len = draw_prompt_len(jax.random.fold_in(seeds[19], 71), 0)
    live_blocks = draw_live_blocks(jax.random.fold_in(seeds[19], 71), 0)
    tail_key = draw_tail_key(jax.random.fold_in(seeds[19], 71), 0)
    tail_value = gaussian(seeds[9], (SAMPLES, PROMPTS, TAIL, D), 3.0, 18.0, ((0, 16), (1, 8)))
    tail_len = draw_tail_len(jax.random.fold_in(seeds[19], 71), 0)
    tail_source = draw_tail_source(jax.random.fold_in(seeds[19], 71), 0)
    routes_keys = jax.random.split(jax.random.fold_in(seeds[12], 1), SAMPLES * PROMPTS * NEW // (PR_DEV * NEW))
    routes_turns = jax.random.permutation(jax.random.fold_in(seeds[12], 3), SAMPLES * PROMPTS * NEW // (PR_DEV * NEW))
    routes = jax.vmap(lambda own, number: assign_block(jax.random.fold_in(seeds[12], 2), own, number, PR_DEV * NEW, EXPERTS, TOP, CAP, 2))(routes_keys, routes_turns).reshape((SAMPLES, PROMPTS, NEW, TOP))
    router = gaussian(seeds[13], (D, EXPERTS), D ** -0.5, 0.125, (), jnp.float32)
    ffn_gain = jnp.clip(1.0 + 0.15 * jax.random.normal(seeds[14], (D,), jnp.float32), 0.25, 1.75)
    w_gate = gaussian(seeds[15], (EXPERTS, D, FF), D ** -0.5, 0.125, ((0, 8), (2, 16)))
    w_up = gaussian(seeds[16], (EXPERTS, D, FF), D ** -0.5, 0.125, ((0, 8), (2, 16)))
    w_down = gaussian(seeds[17], (EXPERTS, FF, D), FF ** -0.5, 0.078125, ((0, 8), (1, 16)))
    score_weight = gaussian(seeds[18], (D,), D ** -0.5, 0.125, (), jnp.float32)
    return {"hidden": hidden, "query": query, "new_key": new_key, "new_value": new_value, "prompt_key": prompt_key, "prompt_value": prompt_value, "prompt_len": prompt_len, "live_blocks": live_blocks, "tail_key": tail_key, "tail_value": tail_value, "tail_len": tail_len, "tail_source": tail_source, "routes": routes, "router": router, "ffn_gain": ffn_gain, "w_gate": w_gate, "w_up": w_up, "w_down": w_down, "score_weight": score_weight}


def attend_prompt(bundle):
    queries, keys_new, values_new, cache_keys, cache_values, tail_keys, tail_values, length_now, page_live, tail_lengths, tail_owner = bundle
    score_scale = HDIM ** (-0.5)
    neg_fill = -1e+30
    query_heads = queries.astype(jnp.float32).reshape(SAMPLES, NEW, HEADS, HDIM)
    cache_kh = cache_keys.astype(jnp.float32).reshape(CTX, HEADS, HDIM)
    cache_vh = cache_values.astype(jnp.float32).reshape(CTX, HEADS, HDIM)
    positions = jnp.arange(CTX)
    cache_usable = (positions < length_now) & (page_live[positions // KVB] > 0)
    cache_scores = jnp.einsum('mthd,chd->mthc', query_heads, cache_kh) * score_scale
    cache_scores = jnp.where(cache_usable[None, None, None, :], cache_scores, neg_fill)
    tail_kh = tail_keys.astype(jnp.float32).reshape(SAMPLES, TAIL, HEADS, HDIM)
    tail_vh = tail_values.astype(jnp.float32).reshape(SAMPLES * TAIL, HEADS, HDIM)
    tail_scores = jnp.einsum('mthd,nuhd->mthnu', query_heads, tail_kh) * score_scale
    samples_idx = jnp.arange(SAMPLES)
    tail_usable = (tail_owner[None, :, None] == samples_idx[:, None, None]) & (jnp.arange(TAIL)[None, None, :] < tail_lengths[:, None, None])
    tail_scores = jnp.where(tail_usable[:, None, None, :, :], tail_scores, neg_fill).reshape(SAMPLES, NEW, HEADS, SAMPLES * TAIL)
    tail_flat = jnp.broadcast_to(tail_usable[:, None, None, :, :], (SAMPLES, NEW, HEADS, SAMPLES, TAIL)).reshape(SAMPLES, NEW, HEADS, SAMPLES * TAIL)
    new_kh = keys_new.astype(jnp.float32).reshape(SAMPLES, NEW, HEADS, HDIM)
    new_vh = values_new.astype(jnp.float32).reshape(SAMPLES, NEW, HEADS, HDIM)
    new_scores = jnp.einsum('mthd,muhd->mthu', query_heads, new_kh) * score_scale
    causal = jnp.arange(NEW)[None, :] <= jnp.arange(NEW)[:, None]
    new_scores = jnp.where(causal[None, :, None, :], new_scores, neg_fill)
    top_score = jnp.maximum(jnp.maximum(lax.optimization_barrier(jnp.max(cache_scores, -1)), lax.optimization_barrier(jnp.max(tail_scores, -1))), lax.optimization_barrier(jnp.max(new_scores, -1)))
    cache_w = jnp.where(cache_usable[None, None, None, :], jnp.exp(cache_scores - top_score[..., None]), 0.0)
    tail_w = jnp.where(tail_flat, jnp.exp(tail_scores - top_score[..., None]), 0.0)
    new_w = jnp.where(causal[None, :, None, :], jnp.exp(new_scores - top_score[..., None]), 0.0)
    denom_sum = lax.optimization_barrier(jnp.sum(cache_w, -1)) + lax.optimization_barrier(jnp.sum(tail_w, -1)) + lax.optimization_barrier(jnp.sum(new_w, -1))
    weighted = jnp.einsum('mthc,chd->mthd', cache_w.astype(jnp.bfloat16).astype(jnp.float32), cache_vh)
    weighted = weighted + jnp.einsum('mthk,khd->mthd', tail_w.astype(jnp.bfloat16).astype(jnp.float32), tail_vh)
    weighted = weighted + jnp.einsum('mthu,muhd->mthd', new_w.astype(jnp.bfloat16).astype(jnp.float32), new_vh)
    return (weighted / denom_sum[..., None]).reshape(SAMPLES, NEW, D)

def reference(hidden, query, new_key, new_value, prompt_key, prompt_value, prompt_len, live_blocks, tail_key, tail_value, tail_len, tail_source, routes, router, ffn_gain, w_gate, w_up, w_down, score_weight):
    bundle = (jnp.swapaxes(query, 0, 1), jnp.swapaxes(new_key, 0, 1), jnp.swapaxes(new_value, 0, 1), prompt_key, prompt_value, jnp.swapaxes(tail_key, 0, 1), jnp.swapaxes(tail_value, 0, 1), prompt_len, live_blocks, tail_len.T, tail_source.T)
    attended = jnp.swapaxes(lax.map(attend_prompt, bundle), 0, 1)
    mixed = hidden.astype(jnp.float32) + attended
    normed = (mixed * lax.rsqrt(lax.optimization_barrier(jnp.mean(mixed * mixed, axis=-1, keepdims=True)) + 1e-05) * ffn_gain).astype(jnp.bfloat16)
    row_count = SAMPLES * PROMPTS * NEW
    flat_rows = normed.reshape(row_count, D)
    chosen = routes.reshape(row_count, TOP)
    logits = jnp.dot(flat_rows.astype(jnp.float32), router, precision=lax.Precision.HIGHEST)
    onehot = (chosen[:, :, None] == jnp.arange(EXPERTS)[None, None, :]).astype(jnp.float32)
    picked = lax.optimization_barrier(jnp.sum(onehot * logits[:, None, :], axis=-1))
    gate_first = 1.0 / (1.0 + jnp.exp(picked[:, 1] - picked[:, 0]))
    gate_second = 1.0 / (1.0 + jnp.exp(picked[:, 0] - picked[:, 1]))
    coefs = gate_first[:, None] * onehot[:, 0] + gate_second[:, None] * onehot[:, 1]

    def expert_step(running, stacked):
        gate_w, up_w, down_w, share = stacked
        gated = jnp.dot(flat_rows, gate_w, preferred_element_type=jnp.float32)
        upward = jnp.dot(flat_rows, up_w, preferred_element_type=jnp.float32)
        activation = (jax.nn.silu(gated) * upward).astype(jnp.bfloat16)
        expert_out = jnp.dot(activation, down_w, preferred_element_type=jnp.float32).astype(jnp.bfloat16)
        return (running + share[:, None] * expert_out.astype(jnp.float32), None)
    moe_sum, _ = lax.scan(expert_step, jnp.zeros((row_count, D), jnp.float32), (w_gate, w_up, w_down, coefs.T))
    layer_out = (mixed.reshape(row_count, D) + moe_sum).astype(jnp.bfloat16)
    score = lax.optimization_barrier(jnp.sum(layer_out.astype(jnp.float32) * score_weight, axis=-1))
    return (layer_out.reshape(SAMPLES, PROMPTS, NEW, D), score.reshape(SAMPLES, PROMPTS, NEW))
```

```python
import jax
import jax.numpy as jnp
from jax import lax
from jax.sharding import PartitionSpec as P

HDIM = 64
TOP = 2
KVB = 16
CAP = 4


neg_fill = -1e30
score_scale = 0.125


def prompt_usable(offset, length, lengths, live_rows):
    page_rows = lax.dynamic_slice_in_dim(live_rows, offset // KVB, length // KVB, 1)
    page_rows = jnp.repeat(page_rows, KVB, axis=1)
    positions = offset + jnp.arange(length)
    return (positions[None, :] < lengths[:, None]) & (page_rows > 0)


def local(
    hidden,
    query,
    new_key,
    new_value,
    prompt_key,
    prompt_value,
    prompt_len,
    live_blocks,
    tail_key,
    tail_value,
    tail_len,
    tail_source,
    routes,
    router,
    ffn_gain,
    w_gate,
    w_up,
    w_down,
    score_weight,
):
    blk_count = lax.axis_size("blk")
    exp_count = lax.axis_size("expert")
    blk_at = lax.axis_index("blk")
    exp_at = lax.axis_index("expert")
    local_prompts = query.shape[1]
    fresh_count = query.shape[2]
    model_width = query.shape[3]
    head_count = model_width // HDIM
    blk_len = prompt_key.shape[1]
    tail_span = tail_key.shape[2]
    my_lengths = lax.dynamic_slice_in_dim(prompt_len, exp_at * local_prompts, local_prompts, 0)
    my_live = lax.dynamic_slice_in_dim(live_blocks, exp_at * local_prompts, local_prompts, 0)
    my_owner = lax.dynamic_slice_in_dim(tail_source, exp_at * local_prompts, local_prompts, 1)
    my_tail_len = lax.dynamic_slice_in_dim(tail_len, exp_at * local_prompts, local_prompts, 1)
    query_heads = query[0].reshape(local_prompts, fresh_count, head_count, HDIM)
    new_heads = new_key[0].reshape(local_prompts, fresh_count, head_count, HDIM)
    new_vheads = new_value[0].reshape(local_prompts, fresh_count, head_count, HDIM)
    causal = jnp.arange(fresh_count)[None, :] <= jnp.arange(fresh_count)[:, None]
    everyone_q = lax.all_to_all(
        jnp.broadcast_to(query, (blk_count, *query.shape[1:])), "blk", 0, 0, tiled=True
    )
    all_heads = everyone_q.reshape(blk_count, local_prompts, fresh_count, head_count, HDIM)
    cache_kh = prompt_key.reshape(local_prompts, blk_len, head_count, HDIM)
    cache_vh = prompt_value.reshape(local_prompts, blk_len, head_count, HDIM)
    cache_ok = prompt_usable(blk_at * blk_len, blk_len, my_lengths, my_live)[None, :, None, None, :]
    cache_scores = (
        jnp.einsum("mpthd,pkhd->mpthk", all_heads, cache_kh, preferred_element_type=jnp.float32)
        * score_scale
    )
    cache_scores = jnp.where(cache_ok, cache_scores, neg_fill)
    slot_kh = tail_key[0].reshape(local_prompts, tail_span, head_count, HDIM)
    slot_vh = tail_value[0].reshape(local_prompts, tail_span, head_count, HDIM)
    owners_here = lax.dynamic_index_in_dim(my_owner, blk_at, 0, keepdims=False)
    slot_ok = (owners_here[None, :] == jnp.arange(blk_count)[:, None])[:, :, None] & (
        jnp.arange(tail_span)[None, None, :] < my_tail_len[:, :, None]
    )
    slot_ok = slot_ok[:, :, None, None, :]
    slot_scores = (
        jnp.einsum("mpthd,pkhd->mpthk", all_heads, slot_kh, preferred_element_type=jnp.float32)
        * score_scale
    )
    slot_scores = jnp.where(slot_ok, slot_scores, neg_fill)
    own_scores = (
        jnp.einsum("pthd,puhd->pthu", query_heads, new_heads, preferred_element_type=jnp.float32)
        * score_scale
    )
    own_scores = jnp.where(causal[None, :, None, :], own_scores, neg_fill)
    local_top = jnp.maximum(jnp.max(cache_scores, axis=-1), jnp.max(slot_scores, axis=-1))
    local_top = jnp.maximum(local_top, -1e4).astype(jnp.bfloat16).astype(jnp.float32)
    cache_w = jnp.where(cache_ok, jnp.exp(cache_scores - local_top[..., None]), 0.0)
    slot_w = jnp.where(slot_ok, jnp.exp(slot_scores - local_top[..., None]), 0.0)
    total = jnp.sum(cache_w, axis=-1) + jnp.sum(slot_w, axis=-1)
    weighted = jnp.einsum(
        "mpthk,pkhd->mpthd",
        cache_w.astype(jnp.bfloat16),
        cache_vh,
        preferred_element_type=jnp.float32,
    )
    weighted = weighted + jnp.einsum(
        "mpthk,pkhd->mpthd",
        slot_w.astype(jnp.bfloat16),
        slot_vh,
        preferred_element_type=jnp.float32,
    )
    total_high = total.astype(jnp.bfloat16)
    total_low = (total - total_high.astype(jnp.float32)).astype(jnp.bfloat16)
    sent = jnp.concatenate(
        [
            weighted.astype(jnp.bfloat16).reshape(blk_count, local_prompts, fresh_count, model_width),
            local_top.astype(jnp.bfloat16),
            total_high,
            total_low,
        ],
        axis=-1,
    )
    sent = sent.reshape(blk_count, local_prompts * fresh_count, -1)
    got = lax.all_to_all(sent, "blk", 0, 0, tiled=True)
    got = got.reshape(blk_count, local_prompts, fresh_count, -1)
    part = got[..., :model_width].astype(jnp.float32)
    part = part.reshape(blk_count, local_prompts, fresh_count, head_count, HDIM)
    stats = got[..., model_width:].astype(jnp.float32)
    part_top = stats[..., :head_count]
    part_total = stats[..., head_count : 2 * head_count] + stats[..., 2 * head_count :]
    own_top = jnp.max(own_scores, axis=-1)
    top = jnp.maximum(jnp.max(part_top, axis=0), own_top)
    rescale = jnp.exp(part_top - top[None])
    own_w = jnp.where(causal[None, :, None, :], jnp.exp(own_scores - top[..., None]), 0.0)
    own_sum = jnp.einsum(
        "pthu,puhd->pthd",
        own_w.astype(jnp.bfloat16),
        new_vheads,
        preferred_element_type=jnp.float32,
    )
    denom = jnp.sum(part_total * rescale, axis=0) + jnp.sum(own_w, axis=-1)
    attended = (jnp.sum(part * rescale[..., None], axis=0) + own_sum) / denom[..., None]
    token_count = local_prompts * fresh_count
    mixed = hidden[0].astype(jnp.float32).reshape(token_count, model_width) + attended.reshape(
        token_count, model_width
    )
    normed = (
        mixed * lax.rsqrt(jnp.mean(mixed * mixed, axis=-1, keepdims=True) + 1e-05) * ffn_gain
    ).astype(jnp.bfloat16)
    chosen = routes[0].reshape(token_count, TOP)
    logits = jnp.dot(normed.astype(jnp.float32), router, precision=lax.Precision.HIGHEST)
    expert_total = router.shape[1]
    onehot = chosen[:, :, None] == jnp.arange(expert_total)[None, None, :]
    picked = jnp.sum(jnp.where(onehot, logits[:, None, :], 0.0), axis=-1)
    gate_first = 1.0 / (1.0 + jnp.exp(picked[:, 1] - picked[:, 0]))
    gate_second = 1.0 / (1.0 + jnp.exp(picked[:, 0] - picked[:, 1]))
    assign_count = token_count * TOP
    assign_hot = onehot.reshape(assign_count, expert_total).astype(jnp.int32)
    earlier = jnp.cumsum(assign_hot, axis=0) - assign_hot
    slot_ids = jnp.sum(earlier * assign_hot, axis=-1)
    assign_expert = chosen.reshape(assign_count)
    local_experts = expert_total // exp_count
    row_ids = jnp.arange(local_experts * exp_count * CAP)
    row_local = row_ids // (exp_count * CAP)
    row_device = row_ids // CAP % exp_count
    row_slot = row_ids % CAP
    row_expert = row_device * local_experts + row_local
    dispatch_map = (
        (row_expert[:, None] == assign_expert[None, :]) & (row_slot[:, None] == slot_ids[None, :])
    ).astype(jnp.bfloat16)
    repeated = jnp.repeat(normed, TOP, axis=0)
    outgoing = jnp.dot(dispatch_map, repeated, preferred_element_type=jnp.float32).astype(
        jnp.bfloat16
    )
    outgoing = outgoing.reshape(local_experts, exp_count, CAP, model_width)
    arrived = lax.all_to_all(outgoing, "expert", split_axis=1, concat_axis=1, tiled=True)
    column_rows = lax.all_to_all(
        jnp.broadcast_to(arrived[None], (blk_count, *arrived.shape)), "blk", 0, 0, tiled=True
    )
    gated = jnp.einsum("nlscd,ldf->nlscf", column_rows, w_gate, preferred_element_type=jnp.float32)
    upward = jnp.einsum("nlscd,ldf->nlscf", column_rows, w_up, preferred_element_type=jnp.float32)
    activation = (jax.nn.silu(gated) * upward).astype(jnp.bfloat16)
    partial_out = jnp.einsum(
        "nlscf,lfd->nlscd", activation, w_down, preferred_element_type=jnp.float32
    ).astype(jnp.bfloat16)
    partial_out = lax.all_to_all(partial_out, "blk", 0, 0, tiled=True)
    summed = jnp.sum(partial_out.astype(jnp.float32), axis=0, keepdims=True).astype(jnp.bfloat16)
    returned = lax.all_to_all(summed, "expert", split_axis=2, concat_axis=2, tiled=True)
    returned = returned.reshape(local_experts * exp_count * CAP, model_width)
    gathered_back = jnp.einsum(
        "ja,jd->ad", dispatch_map, returned, preferred_element_type=jnp.float32
    )
    gathered_back = gathered_back.reshape(token_count, TOP, model_width)
    moe_sum = gate_first[:, None] * gathered_back[:, 0] + gate_second[:, None] * gathered_back[:, 1]
    layer_out = (mixed + moe_sum).astype(jnp.bfloat16)
    score = jnp.sum(layer_out.astype(jnp.float32) * score_weight, axis=-1)
    return (
        layer_out.reshape(1, local_prompts, fresh_count, model_width),
        score.reshape(1, local_prompts, fresh_count),
    )


def solution(mesh):
    placed = (
        P("blk", "expert", None, None),
        P("blk", "expert", None, None),
        P("blk", "expert", None, None),
        P("blk", "expert", None, None),
        P("expert", "blk", None),
        P("expert", "blk", None),
        P(),
        P(),
        P("blk", "expert", None, None),
        P("blk", "expert", None, None),
        P(),
        P(),
        P("blk", "expert", None, None),
        P(),
        P(),
        P("expert", None, "blk"),
        P("expert", None, "blk"),
        P("expert", "blk", None),
        P(),
    )
    return jax.shard_map(
        local,
        mesh=mesh,
        in_specs=placed,
        out_specs=(P("blk", "expert", None, None), P("blk", "expert", None)),
        check_vma=False,
    )
```

```python
import jax
import jax.numpy as jnp
from jax import lax
from jax.experimental import pallas as pl
from jax.experimental.pallas import tpu as pltpu
from jax.sharding import PartitionSpec as P

HDIM = 64
TOP = 2
KVB = 16
CAP = 4
LANES = 128

BF = jnp.bfloat16
F32 = jnp.float32
HIDE = -1e30
FLOOR = -1e4
NT = (((1,), (1,)), ((), ()))


def vmem():
    return pl.BlockSpec(memory_space=pltpu.VMEM)


def smem():
    return pl.BlockSpec(memory_space=pltpu.SMEM)


def iota(shape, dim):
    return lax.broadcasted_iota(jnp.int32, shape, dim)


def dot(a, b, dims=(((1,), (0,)), ((), ()))):
    return lax.dot_general(a, b, dims, preferred_element_type=F32)


def attend_kernel(
    place, lengths, live, tail_len, source, q_ref, k_ref, v_ref, tk_ref, tv_ref, out_ref,
    bias, picks, stat_top, stat_sum,
):
    step = pl.program_id(0)
    prompts, span, width = k_ref.shape
    rows = q_ref.shape[0]
    fresh = 2
    group = prompts * fresh
    samples = rows // group
    heads = out_ref.shape[1] // HDIM - 2
    model = heads * HDIM
    pairs = width // LANES

    @pl.when(step == 0)
    def _():
        blk, exp = place[0], place[1]
        lane = iota((group, LANES), 1)
        sub = iota((group, LANES), 0) // fresh
        ok = jnp.zeros((group, LANES), jnp.int32)
        tail_ok = jnp.zeros((group, LANES), jnp.int32)
        owner = jnp.zeros((group, LANES), jnp.int32)
        for p in range(prompts):
            at = exp * prompts + p
            kept = jnp.zeros((group, LANES), jnp.int32)
            for b in range(span // KVB):
                page = live[at, blk * (span // KVB) + b]
                kept = jnp.where(lane // KVB == b, page, kept)
            left = jnp.minimum(lengths[at] - blk * span, span)
            ok_p = jnp.where(lane < left, jnp.where(kept > 0, 1, 0), 0)
            who = source[blk, at]
            held = tail_len[who, at]
            tail_p = jnp.where(lane >= span, jnp.where(lane - span < held, 1, 0), 0)
            ok = jnp.where(sub == p, ok_p, ok)
            tail_ok = jnp.where(sub == p, tail_p, tail_ok)
            owner = jnp.where(sub == p, who, owner)
        for m in range(samples):
            use = ok + jnp.where(owner == m, tail_ok, 0)
            bias[m * group : (m + 1) * group, :] = jnp.where(use > 0, 0.0, HIDE)
        row_p = (iota((rows, LANES), 0) % group) // fresh
        half = iota((rows, LANES), 1) // HDIM
        for p in range(prompts):
            mine = jnp.where(row_p == p, 1.0, 0.0)
            picks[2 * prompts + p] = mine.astype(BF)
            for h in range(2):
                picks[2 * p + h] = jnp.where(half == h, mine * 0.125, 0.0).astype(BF)
        stat_top[...] = jnp.zeros_like(stat_top)
        stat_sum[...] = jnp.zeros_like(stat_sum)

    lane = iota((rows, LANES), 1)
    hide = jnp.concatenate([bias[...], bias[...]], axis=0)
    for i in range(pairs):
        cut = slice(i * LANES, (i + 1) * LANES)
        pair = step * pairs + i
        q = q_ref[:, cut]
        q_wide = jnp.concatenate(
            [
                jnp.concatenate([q * picks[2 * p], q * picks[2 * p + 1]], axis=0)
                for p in range(prompts)
            ],
            axis=1,
        )
        k_wide = jnp.concatenate(
            [jnp.concatenate([k_ref[p, :, cut], tk_ref[p, :, cut]], axis=0) for p in range(prompts)],
            axis=1,
        )
        scores = dot(q_wide, k_wide, NT) + hide
        top = jnp.maximum(jnp.max(scores, axis=1, keepdims=True), FLOOR)
        top = top.astype(BF).astype(F32)
        weight = jnp.exp(scores - top)
        total = jnp.sum(weight, axis=1, keepdims=True)
        weight = weight.astype(BF)
        w_wide = jnp.concatenate(
            [
                weight * jnp.concatenate([picks[2 * prompts + p], picks[2 * prompts + p]], axis=0)
                for p in range(prompts)
            ],
            axis=1,
        )
        v_high = jnp.concatenate(
            [jnp.concatenate([v_ref[p, :, cut], tv_ref[p, :, cut]], axis=0) for p in range(prompts)],
            axis=0,
        )
        both = dot(w_wide, v_high)
        mixed = jnp.where(lane < HDIM, both[:rows], both[rows:])
        out_ref[:, pl.ds(pl.multiple_of(pair * LANES, LANES), LANES)] = mixed.astype(BF)
        for h in range(2):
            at = 2 * pair + h
            stat_top[...] = jnp.where(lane == at, top[h * rows : (h + 1) * rows], stat_top[...])
            stat_sum[...] = jnp.where(
                lane == heads + at, total[h * rows : (h + 1) * rows], stat_sum[...]
            )

    @pl.when(step == pl.num_programs(0) - 1)
    def _():
        sums = stat_sum[...]
        high = sums.astype(BF).astype(F32)
        low = pltpu.roll(sums - high, heads, 1)
        out_ref[:, model:] = (stat_top[...] + high + low).astype(BF)


def attend(place, lengths, live, tail_len, source, everyone, key, value, tail_key, tail_value):
    rows, model = everyone.shape
    prompts, span, _ = key.shape
    chunk = 3 * LANES
    cache = pl.BlockSpec((prompts, span, chunk), lambda i, *_: (0, 0, i))
    return pl.pallas_call(
        attend_kernel,
        out_shape=jax.ShapeDtypeStruct((rows, model + LANES), BF),
        grid_spec=pltpu.PrefetchScalarGridSpec(
            num_scalar_prefetch=5,
            grid=(model // chunk,),
            in_specs=[pl.BlockSpec((rows, chunk), lambda i, *_: (0, i)), cache, cache, cache, cache],
            out_specs=pl.BlockSpec((rows, model + LANES), lambda i, *_: (0, 0)),
            scratch_shapes=[
                pltpu.VMEM((rows, LANES), F32),
                pltpu.VMEM((3 * prompts, rows, LANES), BF),
                pltpu.VMEM((rows, LANES), F32),
                pltpu.VMEM((rows, LANES), F32),
            ],
        ),
        compiler_params=pltpu.CompilerParams(vmem_limit_bytes=24 << 20),
        name="attend",
    )(place, lengths, live, tail_len, source, everyone, key, value, tail_key, tail_value)


def combine_kernel(
    routes, got_ref, q_ref, k_ref, v_ref, h_ref, router_ref, gain_ref,
    mixed_ref, rows_ref, gate_ref, q8, k0, k1, v0, v1, spread,
):
    parts, tokens, wide = got_ref.shape
    model = wide - LANES
    heads = model // HDIM
    prompts, fresh = q_ref.shape[1], q_ref.shape[2]
    experts = router_ref.shape[0]
    for p in range(prompts):
        at = slice(fresh * p, fresh * (p + 1))
        q8[at, :] = q_ref[0, p].astype(F32)
        mixed_ref[at, :] = h_ref[0, p].astype(F32)
        key, val = k_ref[0, p].astype(F32), v_ref[0, p].astype(F32)
        k0[at, :] = jnp.broadcast_to(key[0:1], (fresh, model))
        k1[at, :] = jnp.broadcast_to(key[1:2], (fresh, model))
        v0[at, :] = jnp.broadcast_to(val[0:1], (fresh, model))
        v1[at, :] = jnp.broadcast_to(val[1:2], (fresh, model))
    spread[...] = jnp.where(
        iota((LANES, model), 1) // HDIM == iota((LANES, model), 0), 1.0, 0.0
    ).astype(BF)
    product = jnp.concatenate([q8[...] * k0[...], q8[...] * k1[...]], axis=0)
    high = product.astype(BF)
    low = (product - high.astype(F32)).astype(BF)
    own = (dot(high, spread[...], NT) + dot(low, spread[...], NT)) * 0.125
    lane = iota((tokens, LANES), 1)
    sub = iota((tokens, LANES), 0)
    s0 = own[:tokens]
    s1 = jnp.where(sub % fresh == 1, own[tokens:], HIDE)
    top = jnp.maximum(s0, s1)
    tops, sums = [], []
    for j in range(parts):
        stat = got_ref[j, :, model:].astype(F32)
        tops.append(jnp.where(lane < heads, stat, 0.0))
        total = pltpu.roll(stat, LANES - heads, 1) + pltpu.roll(stat, LANES - 2 * heads, 1)
        sums.append(jnp.where(lane < heads, total, 1.0))
        top = jnp.maximum(top, tops[-1])
    w0, w1 = jnp.exp(s0 - top), jnp.exp(s1 - top)
    scale = [jnp.exp(t - top) for t in tops]
    total = w0 + w1
    for c, l in zip(scale, sums):
        total = total + c * l
    inverse = 1.0 / total
    share = jnp.concatenate([c * inverse for c in scale] + [w0 * inverse, w1 * inverse], axis=0)
    share_high = share.astype(BF)
    share_low = (share - share_high.astype(F32)).astype(BF)
    square = jnp.zeros((tokens, LANES), F32)
    chunk = 2 * LANES
    for c in range(model // chunk):
        cut = slice(c * chunk, (c + 1) * chunk)
        each = dot(share_high, spread[:, cut]) + dot(share_low, spread[:, cut])
        here = mixed_ref[:, cut]
        for j in range(parts):
            here = here + each[j * tokens : (j + 1) * tokens] * got_ref[j, :, cut].astype(F32)
        here = here + each[parts * tokens : (parts + 1) * tokens] * v0[:, cut]
        here = here + each[(parts + 1) * tokens :] * v1[:, cut]
        mixed_ref[:, cut] = here
        for i in range(chunk // LANES):
            part = here[:, i * LANES : (i + 1) * LANES]
            square = square + part * part
    mean = jnp.sum(square, axis=1, keepdims=True) / model
    normed = (mixed_ref[...] * lax.rsqrt(mean + 1e-05) * gain_ref[...]).astype(BF).astype(F32)
    logits = [jnp.sum(normed * router_ref[e : e + 1, :], axis=1, keepdims=True) for e in range(experts)]
    token = iota((tokens, 1), 0)
    first = jnp.zeros((tokens, 1), jnp.int32)
    second = jnp.zeros((tokens, 1), jnp.int32)
    slots = experts * CAP
    row = iota((slots, tokens), 0)
    column = iota((slots, tokens), 1)
    pick = jnp.zeros((slots, tokens), F32)
    seen = jnp.zeros((slots, tokens), jnp.int32)
    for i in range(tokens):
        pair = [routes[0, i // fresh, i % fresh, r] for r in range(TOP)]
        first = jnp.where(token == i, pair[0], first)
        second = jnp.where(token == i, pair[1], second)
        for expert in pair:
            match = row // CAP == expert
            hit = jnp.where(match, jnp.where(column == i, jnp.where(row % CAP == seen, 1.0, 0.0), 0.0), 0.0)
            pick = pick + hit
            seen = seen + jnp.where(match, 1, 0)
    logit0 = jnp.zeros((tokens, 1), F32)
    logit1 = jnp.zeros((tokens, 1), F32)
    for e in range(experts):
        logit0 = jnp.where(first == e, logits[e], logit0)
        logit1 = jnp.where(second == e, logits[e], logit1)
    gate0 = 1.0 / (1.0 + jnp.exp(logit1 - logit0))
    gate1 = 1.0 / (1.0 + jnp.exp(logit0 - logit1))
    gate_ref[...] = jnp.where(lane == 0, gate0, jnp.where(lane == 1, gate1, 0.0))
    outgoing = dot(pick, normed).astype(BF)
    for e in range(experts):
        rows_ref[e] = outgoing[e * CAP : (e + 1) * CAP]


def combine(routes, got, query, new_key, new_value, hidden, router, gain):
    parts, tokens, wide = got.shape
    model = wide - LANES
    experts = router.shape[0]
    return pl.pallas_call(
        combine_kernel,
        out_shape=(
            jax.ShapeDtypeStruct((tokens, model), F32),
            jax.ShapeDtypeStruct((experts, CAP, model), BF),
            jax.ShapeDtypeStruct((tokens, LANES), F32),
        ),
        in_specs=[smem()] + [vmem()] * 7,
        out_specs=(vmem(), vmem(), vmem()),
        scratch_shapes=[pltpu.VMEM((tokens, model), F32)] * 5 + [pltpu.VMEM((LANES, model), BF)],
        compiler_params=pltpu.CompilerParams(vmem_limit_bytes=16 << 20),
        name="combine",
    )(routes, got, query, new_key, new_value, hidden, router, gain)


def ffn_kernel(x_ref, gate_ref, up_ref, down_ref, out_ref):
    x = x_ref[...]
    gated = dot(x, gate_ref[...], NT)
    upward = dot(x, up_ref[...], NT)
    activation = (gated / (1.0 + jnp.exp(-gated)) * upward).astype(BF)
    out_ref[...] = dot(activation, down_ref[...]).astype(BF)


def ffn(x, w_gate, w_up, w_down):
    rows, model = x.shape
    units = w_down.shape[0]
    step = 128
    whole = pl.BlockSpec((units, model), lambda i: (0, 0))
    moving = pl.BlockSpec((step, model), lambda i: (i, 0))
    return pl.pallas_call(
        ffn_kernel,
        out_shape=jax.ShapeDtypeStruct((rows, model), BF),
        grid=(rows // step,),
        in_specs=[moving, whole, whole, whole],
        out_specs=moving,
        compiler_params=pltpu.CompilerParams(vmem_limit_bytes=24 << 20),
        name="ffn",
    )(x, w_gate, w_up, w_down)


def finish_kernel(routes, back_ref, mixed_ref, gate_ref, weight_ref, out_ref, score_ref, whole):
    slots, model = whole.shape
    tokens = mixed_ref.shape[0]
    prompts, fresh = out_ref.shape[1], out_ref.shape[2]
    for e in range(slots // CAP):
        whole[e * CAP : (e + 1) * CAP, :] = back_ref[e].astype(F32)
    row = iota((tokens, slots), 0)
    column = iota((tokens, slots), 1)
    seen = jnp.zeros((tokens, slots), jnp.int32)
    picks = [jnp.zeros((tokens, slots), F32) for _ in range(TOP)]
    for i in range(tokens):
        for r in range(TOP):
            match = column // CAP == routes[0, i // fresh, i % fresh, r]
            hit = jnp.where(match, jnp.where(row == i, jnp.where(column % CAP == seen, 1.0, 0.0), 0.0), 0.0)
            picks[r] = picks[r] + hit
            seen = seen + jnp.where(match, 1, 0)
    every = whole[...]
    total = mixed_ref[...]
    for r in range(TOP):
        total = total + gate_ref[:, r : r + 1] * dot(picks[r], every)
    done = total.astype(BF)
    score_ref[...] = jnp.sum(done.astype(F32) * weight_ref[...], axis=1, keepdims=True)
    for p in range(prompts):
        out_ref[0, p] = done[fresh * p : fresh * (p + 1)]


def finish(routes, back, mixed, gates, weight):
    tokens, model = mixed.shape
    prompts, fresh = routes.shape[1], routes.shape[2]
    return pl.pallas_call(
        finish_kernel,
        out_shape=(
            jax.ShapeDtypeStruct((1, prompts, fresh, model), BF),
            jax.ShapeDtypeStruct((tokens, 1), F32),
        ),
        in_specs=[smem()] + [vmem()] * 4,
        out_specs=(vmem(), vmem()),
        scratch_shapes=[pltpu.VMEM((back.shape[0] * CAP, model), F32)],
        compiler_params=pltpu.CompilerParams(vmem_limit_bytes=16 << 20),
        name="finish",
    )(routes, back, mixed, gates, weight)


def exchange(x, axis):
    return lax.all_to_all(x, axis, 0, 0, tiled=True)


def local(
    hidden,
    query,
    new_key,
    new_value,
    prompt_key,
    prompt_value,
    prompt_len,
    live_blocks,
    tail_key,
    tail_value,
    tail_len,
    tail_source,
    routes,
    router,
    ffn_gain,
    w_gate,
    w_up,
    w_down,
    score_weight,
):
    blk_count = lax.axis_size("blk")
    place = jnp.stack([lax.axis_index("blk"), lax.axis_index("expert")])
    prompts, fresh, model = query.shape[1:]
    tokens = prompts * fresh
    own = query.reshape(1, tokens, model)
    everyone = exchange(jnp.broadcast_to(own, (blk_count, tokens, model)), "blk")
    sent = attend(
        place,
        prompt_len,
        live_blocks,
        tail_len,
        tail_source,
        everyone.reshape(blk_count * tokens, model),
        prompt_key,
        prompt_value,
        tail_key[0],
        tail_value[0],
    )
    got = exchange(sent.reshape(blk_count, tokens, -1), "blk")
    mixed, outgoing, gates = combine(
        routes, got, query, new_key, new_value, hidden, router.T, ffn_gain[None]
    )
    arrived = exchange(outgoing, "expert")
    arrived = arrived.reshape(1, -1, model)
    rows = exchange(jnp.broadcast_to(arrived, (blk_count, *arrived.shape[1:])), "blk")
    partial = ffn(rows.reshape(-1, model), w_gate[0].T, w_up[0].T, w_down[0])
    partial = exchange(partial.reshape(rows.shape), "blk")
    summed = jnp.sum(partial.astype(F32), axis=0).astype(BF)
    back = exchange(summed.reshape(outgoing.shape), "expert")
    layer_out, score = finish(routes, back, mixed, gates, score_weight[None])
    return layer_out, score.reshape(1, prompts, fresh)


def solution(mesh):
    token = P("blk", "expert", None, None)
    cache = P("expert", "blk", None)
    columns = P("expert", None, "blk")
    placed = (
        token, token, token, token, cache, cache, P(), P(), token, token, P(), P(), token, P(), P(),
        columns, columns, cache, P(),
    )
    return jax.shard_map(
        local,
        mesh=mesh,
        in_specs=placed,
        out_specs=(token, P("blk", "expert", None)),
        check_vma=False,
    )
```

```python
import jax
import jax.numpy as jnp
from jax import lax
from jax.experimental import pallas as pl
from jax.experimental.pallas import tpu as pltpu
from jax.sharding import PartitionSpec as P

HDIM = 64
TOP = 2
KVB = 16
CAP = 4
LANES = 128
ROOM = 61 << 20

BF = jnp.bfloat16
F32 = jnp.float32
HIDE = -1e30
FLOOR = -1e4
NT = (((1,), (1,)), ((), ()))


def vmem():
    return pl.BlockSpec(memory_space=pltpu.VMEM)


def smem():
    return pl.BlockSpec(memory_space=pltpu.SMEM)


def iota(shape, dim):
    return lax.broadcasted_iota(jnp.int32, shape, dim)


def dot(a, b, dims=(((1,), (0,)), ((), ()))):
    return lax.dot_general(a, b, dims, preferred_element_type=F32)


def share_kernel(q_ref, out_ref, flat):
    prompts, fresh = q_ref.shape[1], q_ref.shape[2]
    for p in range(prompts):
        flat[fresh * p : fresh * (p + 1), :] = q_ref[0, p].astype(F32) * 0.125
    rows = flat[...].astype(BF)
    for m in range(out_ref.shape[0]):
        out_ref[m] = rows


def share(query, samples):
    _, prompts, fresh, model = query.shape
    tokens = prompts * fresh
    return pl.pallas_call(
        share_kernel,
        out_shape=jax.ShapeDtypeStruct((samples, tokens, model), BF),
        in_specs=[vmem()],
        out_specs=vmem(),
        scratch_shapes=[pltpu.VMEM((tokens, model), F32)],
        compiler_params=pltpu.CompilerParams(vmem_limit_bytes=16 << 20),
        name="share",
    )(query)


def attend_kernel(
    lengths, live, tail_len, source, q_ref, k_ref, tk_hbm, v_hbm, tv_hbm, out_ref,
    tk_buf, v_buf, tv_buf, rows_in, rows_out, stats_in, score_buf, weight_buf, sems,
):
    prompts, span, model = k_ref.shape
    rows = q_ref.shape[0]
    fresh = 2
    group = prompts * fresh
    samples = rows // group
    each = fresh * samples
    heads = model // HDIM
    pairs = model // LANES
    blk, exp = lax.axis_index("blk"), lax.axis_index("expert")
    moves = ((tk_hbm, tk_buf), (v_hbm, v_buf), (tv_hbm, tv_buf))

    def copy(p, i):
        src, dst = moves[i]
        return pltpu.make_async_copy(src.at[p], dst.at[p], sems.at[p, i])

    for p in range(prompts):
        for i in range(len(moves)):
            copy(p, i).start()
    for i in range(pairs):
        rows_in[i] = q_ref[:, i * LANES : (i + 1) * LANES].astype(F32)
    lane = iota((each, LANES), 1)
    sample = iota((each, LANES), 0) % samples

    @pl.loop(0, prompts)
    def _(p):
        at = exp * prompts + p
        kept = jnp.zeros((each, LANES), jnp.int32)
        for b in range(span // KVB):
            kept = jnp.where(lane // KVB == b, live[at, blk * (span // KVB) + b], kept)
        left = jnp.minimum(lengths[at] - blk * span, span)
        prompt_ok = jnp.where(lane < left, jnp.where(kept > 0, 1, 0), 0)
        who = source[blk, at]
        held = tail_len[who, at]
        tail_ok = jnp.where(lane >= span, jnp.where(lane - span < held, 1, 0), 0)
        use = prompt_ok + jnp.where(sample == who, tail_ok, 0)
        hide = jnp.where(use > 0, 0.0, HIDE)
        hide = jnp.concatenate([hide, hide], axis=0)
        copy(p, 0).wait()
        tops = jnp.zeros((each, LANES), F32)
        sums = jnp.zeros((each, LANES), F32)
        for i in range(pairs):
            cut = slice(i * LANES, (i + 1) * LANES)
            q = jnp.concatenate(
                [rows_in[i, pl.ds(fresh * p + t, samples, stride=group), :] for t in range(fresh)],
                axis=0,
            )
            q = jnp.concatenate([jnp.where(lane < HDIM, q, 0.0), jnp.where(lane < HDIM, 0.0, q)], axis=0)
            score_buf[i] = dot(
                q.astype(BF), jnp.concatenate([k_ref[p, :, cut], tk_buf[p, :, cut]], axis=0), NT
            ) + hide
        for i in range(pairs):
            scores = score_buf[i]
            top = jnp.maximum(jnp.max(scores, axis=1, keepdims=True), FLOOR)
            top = top.astype(BF).astype(F32)
            weight = jnp.exp(scores - top)
            total = jnp.sum(weight, axis=1, keepdims=True)
            weight_buf[i] = weight.astype(BF)
            for h in range(2):
                part = slice(h * each, (h + 1) * each)
                tops = jnp.where(lane == 2 * i + h, top[part], tops)
                sums = jnp.where(lane == heads + 2 * i + h, total[part], sums)
        copy(p, 1).wait()
        copy(p, 2).wait()
        for i in range(pairs):
            cut = slice(i * LANES, (i + 1) * LANES)
            val = jnp.concatenate([v_buf[p, :, cut], tv_buf[p, :, cut]], axis=0)
            both = dot(weight_buf[i], val)
            mixed = jnp.where(lane < HDIM, both[:each], both[each:])
            for t in range(fresh):
                rows_out[i, pl.ds(fresh * p + t, samples, stride=group), :] = mixed[
                    t * samples : (t + 1) * samples
                ]
        high = sums.astype(BF).astype(F32)
        stats = tops + high + pltpu.roll(sums - high, heads, 1)
        for t in range(fresh):
            stats_in[pl.ds(fresh * p + t, samples, stride=group), :] = stats[
                t * samples : (t + 1) * samples
            ]

    for i in range(pairs):
        out_ref[:, i * LANES : (i + 1) * LANES] = rows_out[i].astype(BF)
    out_ref[:, model:] = stats_in[...].astype(BF)


def attend(lengths, live, tail_len, source, everyone, key, tail_key, value, tail_value):
    rows, model = everyone.shape
    prompts, span, _ = key.shape
    pairs = model // LANES
    cache = pltpu.VMEM((prompts, span, model), BF)
    where = pl.BlockSpec(memory_space=pl.ANY)
    return pl.pallas_call(
        attend_kernel,
        out_shape=jax.ShapeDtypeStruct((rows, model + LANES), BF),
        in_specs=[smem()] * 4 + [vmem()] * 2 + [where] * 3,
        out_specs=vmem(),
        scratch_shapes=[
            cache,
            cache,
            cache,
            pltpu.VMEM((pairs, rows, LANES), F32),
            pltpu.VMEM((pairs, rows, LANES), F32),
            pltpu.VMEM((rows, LANES), F32),
            pltpu.VMEM((pairs, 2 * rows // prompts, LANES), F32),
            pltpu.VMEM((pairs, 2 * rows // prompts, LANES), BF),
            pltpu.SemaphoreType.DMA((prompts, 3)),
        ],
        compiler_params=pltpu.CompilerParams(vmem_limit_bytes=ROOM),
        name="attend",
    )(lengths, live, tail_len, source, everyone, key, tail_key, value, tail_value)


def row_of(expert, core):
    away = jnp.where(expert % 2 == core, 0, CAP)
    return expert // 2 * (2 * CAP) + away


def combine_kernel(
    routes, got_ref, q_ref, k_ref, v_ref, h_ref, router_ref, gain_ref,
    mixed_ref, rows_ref, gate_ref, q8, k0, k1, v0, v1, spread,
):
    parts, tokens, wide = got_ref.shape
    model = wide - LANES
    heads = model // HDIM
    prompts, fresh = q_ref.shape[1], q_ref.shape[2]
    experts = router_ref.shape[0]
    for p in range(prompts):
        at = slice(fresh * p, fresh * (p + 1))
        q8[at, :] = q_ref[0, p].astype(F32)
        mixed_ref[at, :] = h_ref[0, p].astype(F32)
        key, val = k_ref[0, p].astype(F32), v_ref[0, p].astype(F32)
        k0[at, :] = jnp.broadcast_to(key[0:1], (fresh, model))
        k1[at, :] = jnp.broadcast_to(key[1:2], (fresh, model))
        v0[at, :] = jnp.broadcast_to(val[0:1], (fresh, model))
        v1[at, :] = jnp.broadcast_to(val[1:2], (fresh, model))
    spread[...] = jnp.where(
        iota((LANES, model), 1) // HDIM == iota((LANES, model), 0), 1.0, 0.0
    ).astype(BF)
    product = jnp.concatenate([q8[...] * k0[...], q8[...] * k1[...]], axis=0)
    high = product.astype(BF)
    low = (product - high.astype(F32)).astype(BF)
    own = (dot(high, spread[...], NT) + dot(low, spread[...], NT)) * 0.125
    lane = iota((tokens, LANES), 1)
    sub = iota((tokens, LANES), 0)
    s0 = own[:tokens]
    s1 = jnp.where(sub % fresh == 1, own[tokens:], HIDE)
    top = jnp.maximum(s0, s1)
    tops, sums = [], []
    for j in range(parts):
        stat = got_ref[j, :, model:].astype(F32)
        tops.append(jnp.where(lane < heads, stat, 0.0))
        total = pltpu.roll(stat, LANES - heads, 1) + pltpu.roll(stat, LANES - 2 * heads, 1)
        sums.append(jnp.where(lane < heads, total, 1.0))
        top = jnp.maximum(top, tops[-1])
    w0, w1 = jnp.exp(s0 - top), jnp.exp(s1 - top)
    scale = [jnp.exp(t - top) for t in tops]
    total = w0 + w1
    for c, l in zip(scale, sums):
        total = total + c * l
    inverse = 1.0 / total
    share = jnp.concatenate([c * inverse for c in scale] + [w0 * inverse, w1 * inverse], axis=0)
    share_high = share.astype(BF)
    share_low = (share - share_high.astype(F32)).astype(BF)
    square = jnp.zeros((tokens, LANES), F32)
    chunk = 2 * LANES
    for c in range(model // chunk):
        cut = slice(c * chunk, (c + 1) * chunk)
        each = dot(share_high, spread[:, cut]) + dot(share_low, spread[:, cut])
        here = mixed_ref[:, cut]
        for j in range(parts):
            here = here + each[j * tokens : (j + 1) * tokens] * got_ref[j, :, cut].astype(F32)
        here = here + each[parts * tokens : (parts + 1) * tokens] * v0[:, cut]
        here = here + each[(parts + 1) * tokens :] * v1[:, cut]
        mixed_ref[:, cut] = here
        for i in range(chunk // LANES):
            part = here[:, i * LANES : (i + 1) * LANES]
            square = square + part * part
    mean = jnp.sum(square, axis=1, keepdims=True) / model
    scale = lax.rsqrt(mean + 1e-05)
    normed = jnp.concatenate(
        [
            mixed_ref[:, i * LANES : (i + 1) * LANES] * scale * gain_ref[i : i + 1, :]
            for i in range(model // LANES)
        ],
        axis=1,
    )
    normed = normed.astype(BF).astype(F32)
    logits = [jnp.sum(normed * router_ref[e : e + 1, :], axis=1, keepdims=True) for e in range(experts)]
    token = iota((tokens, 1), 0)
    first = jnp.zeros((tokens, 1), jnp.int32)
    second = jnp.zeros((tokens, 1), jnp.int32)
    slots = experts * CAP
    core = lax.axis_index("expert") % 2
    row = iota((slots, tokens), 0)
    column = iota((slots, tokens), 1)
    pick = jnp.zeros((slots, tokens), F32)
    seen = jnp.zeros((slots, tokens), jnp.int32)
    for i in range(tokens):
        pair = [routes[i % fresh, r, i // fresh] for r in range(TOP)]
        first = jnp.where(token == i, pair[0], first)
        second = jnp.where(token == i, pair[1], second)
        for expert in pair:
            match = row // CAP * CAP == row_of(expert, core)
            hit = jnp.where(match, jnp.where(column == i, jnp.where(row % CAP == seen, 1.0, 0.0), 0.0), 0.0)
            pick = pick + hit
            seen = seen + jnp.where(match, 1, 0)
    logit0 = jnp.zeros((tokens, 1), F32)
    logit1 = jnp.zeros((tokens, 1), F32)
    for e in range(experts):
        logit0 = jnp.where(first == e, logits[e], logit0)
        logit1 = jnp.where(second == e, logits[e], logit1)
    gate0 = 1.0 / (1.0 + jnp.exp(logit1 - logit0))
    gate1 = 1.0 / (1.0 + jnp.exp(logit0 - logit1))
    gate_ref[...] = jnp.where(lane == 0, gate0, jnp.where(lane == 1, gate1, 0.0))
    rows_ref[...] = dot(pick, normed).astype(BF)


def combine(routes, got, query, new_key, new_value, hidden, router, gain):
    parts, tokens, wide = got.shape
    model = wide - LANES
    experts = router.shape[0]
    return pl.pallas_call(
        combine_kernel,
        out_shape=(
            jax.ShapeDtypeStruct((tokens, model), F32),
            jax.ShapeDtypeStruct((experts * CAP, model), BF),
            jax.ShapeDtypeStruct((tokens, LANES), F32),
        ),
        in_specs=[smem()] + [vmem()] * 7,
        out_specs=(vmem(), vmem(), vmem()),
        scratch_shapes=[pltpu.VMEM((tokens, model), F32)] * 5 + [pltpu.VMEM((LANES, model), BF)],
        compiler_params=pltpu.CompilerParams(vmem_limit_bytes=16 << 20),
        name="combine",
    )(routes, got, query, new_key, new_value, hidden, router, gain)


def ffn_kernel(x_ref, gate_ref, up_ref, down_ref, out_ref):
    x = x_ref[...]
    gated = dot(x, gate_ref[...], NT)
    upward = dot(x, up_ref[...], NT)
    activation = (gated / (1.0 + jnp.exp(-gated)) * upward).astype(BF)
    out_ref[...] = dot(activation, down_ref[...]).astype(BF)


def ffn(x, w_gate, w_up, w_down):
    return pl.pallas_call(
        ffn_kernel,
        out_shape=jax.ShapeDtypeStruct(x.shape, BF),
        in_specs=[vmem()] * 4,
        out_specs=vmem(),
        compiler_params=pltpu.CompilerParams(vmem_limit_bytes=16 << 20),
        cost_estimate=pl.CostEstimate(
            flops=6 * x.size * w_gate.shape[0],
            bytes_accessed=2 * (2 * x.size + 3 * w_gate.size),
            transcendentals=x.shape[0] * w_gate.shape[0],
        ),
        name="ffn",
    )(x, w_gate, w_up, w_down)


def finish_kernel(routes, mine_ref, back_ref, mixed_ref, gate_ref, weight_ref, out_ref, score_ref):
    slots, model = mine_ref.shape
    tokens = mixed_ref.shape[0]
    prompts, fresh = out_ref.shape[1], out_ref.shape[2]
    near = iota((slots, model), 0) % (2 * CAP) < CAP
    every = jnp.where(near, mine_ref[...].astype(F32), back_ref[...].astype(F32))
    core = lax.axis_index("expert") % 2
    row = iota((tokens, slots), 0)
    column = iota((tokens, slots), 1)
    seen = jnp.zeros((tokens, slots), jnp.int32)
    picks = [jnp.zeros((tokens, slots), F32) for _ in range(TOP)]
    for i in range(tokens):
        for r in range(TOP):
            match = column // CAP * CAP == row_of(routes[i % fresh, r, i // fresh], core)
            hit = jnp.where(match, jnp.where(row == i, jnp.where(column % CAP == seen, 1.0, 0.0), 0.0), 0.0)
            picks[r] = picks[r] + hit
            seen = seen + jnp.where(match, 1, 0)
    total = mixed_ref[...]
    for r in range(TOP):
        total = total + gate_ref[:, r : r + 1] * dot(picks[r], every)
    done = total.astype(BF)
    kept = done.astype(F32)
    partial = jnp.zeros((tokens, LANES), F32)
    for i in range(model // LANES):
        partial = partial + kept[:, i * LANES : (i + 1) * LANES] * weight_ref[i : i + 1, :]
    score = jnp.sum(partial, axis=1, keepdims=True)
    token = iota((tokens, LANES), 0)
    score = jnp.where(token // fresh == iota((tokens, LANES), 1), score, 0.0)
    for t in range(fresh):
        line = jnp.sum(jnp.where(token % fresh == t, score, 0.0), axis=0, keepdims=True)
        score_ref[t : t + 1, :] = line[:, :prompts]
    for p in range(prompts):
        out_ref[0, p] = done[fresh * p : fresh * (p + 1)]


def finish(routes, mine, back, mixed, gates, weight):
    tokens, model = mixed.shape
    fresh, _, prompts = routes.shape
    return pl.pallas_call(
        finish_kernel,
        out_shape=(
            jax.ShapeDtypeStruct((1, prompts, fresh, model), BF),
            jax.ShapeDtypeStruct((fresh, prompts), F32),
        ),
        in_specs=[smem()] + [vmem()] * 5,
        out_specs=(vmem(), vmem()),
        compiler_params=pltpu.CompilerParams(vmem_limit_bytes=16 << 20),
        name="finish",
    )(routes, mine, back, mixed, gates, weight)


def exchange(x, axis):
    return lax.all_to_all(x, axis, 0, 0, tiled=True)


def local(
    hidden,
    query,
    new_key,
    new_value,
    prompt_key,
    prompt_value,
    prompt_len,
    live_blocks,
    tail_key,
    tail_value,
    tail_len,
    tail_source,
    routes,
    router,
    ffn_gain,
    w_gate,
    w_up,
    w_down,
    score_weight,
):
    blk_count = lax.axis_size("blk")
    prompts, fresh, model = query.shape[1:]
    tokens = prompts * fresh
    everyone = exchange(share(query, blk_count), "blk")
    chosen = routes[0].transpose(1, 2, 0)
    sent = attend(
        prompt_len,
        live_blocks,
        tail_len,
        tail_source,
        everyone.reshape(blk_count * tokens, model),
        prompt_key,
        tail_key[0],
        prompt_value,
        tail_value[0],
    )
    got = exchange(sent.reshape(blk_count, tokens, -1), "blk")
    mixed, outgoing, gates = combine(
        chosen, got, query, new_key, new_value, hidden, router.T, ffn_gain.reshape(-1, LANES)
    )
    exp_count = lax.axis_size("expert")
    both = ("blk", "expert")
    side = 4
    planes = exp_count // 2
    device = lambda x, z, y, c: (x * side + z) * exp_count + y * 2 + c
    swap = [(i, i ^ 1) for i in range(exp_count)]
    lines = [
        [device(o, k, y, 0) if c == 0 else device(k, o, y, 1) for k in range(side) for y in range(planes)]
        for c in range(2)
        for o in range(side)
    ]

    def shift(step):
        moves = []
        for x in range(side):
            for z in range(side):
                for y in range(planes):
                    moves.append((device(x, z, y, 0), device((x + step) % side, z, y, 0)))
                    moves.append((device(x, z, y, 1), device(x, (z + step) % side, y, 1)))
        return moves

    wide = (planes, 2 * CAP, model)
    near = jnp.arange(2 * CAP)[None, :, None] < CAP
    rows = jnp.where(
        near, outgoing.reshape(wide), lax.ppermute(outgoing, "expert", swap).reshape(wide)
    )
    rows = jnp.broadcast_to(rows[None], (side, *wide)).reshape(-1, 2 * CAP, model)
    rows = lax.all_to_all(rows, both, 0, 0, tiled=True, axis_index_groups=lines)
    rows = rows.reshape(-1, model)
    weights = (w_gate[0].T, w_up[0].T, w_down[0])
    order = (2, 1, 3)
    arrivals = [lax.ppermute(rows, both, shift(s)) for s in order]
    total = ffn(rows, *weights)
    parts = [total]
    for s, arrived in zip(order, arrivals):
        arrived, parts[0] = lax.optimization_barrier((arrived, parts[0]))
        parts.append(lax.ppermute(ffn(arrived, *weights), both, shift(-s)))
    total = sum(part.astype(F32) for part in parts).astype(BF)
    total = lax.all_to_all(
        total.reshape(-1, 2 * CAP, model), both, 0, 0, tiled=True, axis_index_groups=lines
    )
    total = total.reshape(side, -1, model)
    mine = jnp.sum(total.astype(F32), axis=0).astype(BF)
    back = lax.ppermute(mine, "expert", swap)
    layer_out, score = finish(chosen, mine, back, mixed, gates, score_weight.reshape(-1, LANES))
    return layer_out, score.T[None]


def solution(mesh):
    token = P("blk", "expert", None, None)
    cache = P("expert", "blk", None)
    columns = P("expert", None, "blk")
    placed = (
        token, token, token, token, cache, cache, P(), P(), token, token, P(), P(), token, P(), P(),
        columns, columns, cache, P(),
    )
    return jax.shard_map(
        local,
        mesh=mesh,
        in_specs=placed,
        out_specs=(token, P("blk", "expert", None)),
        check_vma=False,
    )
```

```python
import jax
import jax.numpy as jnp
from jax import lax
from jax.experimental import pallas as pl
from jax.experimental.pallas import tpu as pltpu
from jax.sharding import PartitionSpec as P

HDIM = 64
TOP = 2
KVB = 16
CAP = 4
LANES = 128
ROOM = 51 << 20

BF = jnp.bfloat16
F32 = jnp.float32
HIDE = -1e30
FLOOR = -1e4
NT = (((1,), (1,)), ((), ()))


def vmem():
    return pl.BlockSpec(memory_space=pltpu.VMEM)


def smem():
    return pl.BlockSpec(memory_space=pltpu.SMEM)


def iota(shape, dim):
    return lax.broadcasted_iota(jnp.int32, shape, dim)


def dot(a, b, dims=(((1,), (0,)), ((), ()))):
    return lax.dot_general(a, b, dims, preferred_element_type=F32)


def share_kernel(q_ref, out_ref, flat):
    prompts, fresh = q_ref.shape[1], q_ref.shape[2]
    for p in range(prompts):
        flat[fresh * p : fresh * (p + 1), :] = q_ref[0, p].astype(F32) * 0.125
    rows = flat[...].astype(BF)
    for m in range(out_ref.shape[0]):
        out_ref[m] = rows


def share(query, samples):
    _, prompts, fresh, model = query.shape
    tokens = prompts * fresh
    return pl.pallas_call(
        share_kernel,
        out_shape=jax.ShapeDtypeStruct((samples, tokens, model), BF),
        in_specs=[vmem()],
        out_specs=vmem(),
        scratch_shapes=[pltpu.VMEM((tokens, model), F32)],
        compiler_params=pltpu.CompilerParams(vmem_limit_bytes=16 << 20),
        name="share",
    )(query)


def attend_kernel(
    lengths, live, tail_len, source, q_ref, k_ref, tk_hbm, v_hbm, tv_hbm, out_ref,
    tk_buf, v_buf, tv_buf, rows_in, rows_out, stats_in, score_buf, weight_buf, sems,
):
    prompts, span, model = k_ref.shape
    rows = q_ref.shape[0]
    fresh = 2
    group = prompts * fresh
    samples = rows // group
    each = fresh * samples
    heads = model // HDIM
    pairs = model // LANES
    blk, exp = lax.axis_index("blk"), lax.axis_index("expert")
    moves = ((tk_hbm, tk_buf), (v_hbm, v_buf), (tv_hbm, tv_buf))

    def copy(p, i):
        src, dst = moves[i]
        return pltpu.make_async_copy(src.at[p], dst.at[p], sems.at[p, i])

    for p in range(prompts):
        for i in range(len(moves)):
            copy(p, i).start()
    for i in range(pairs):
        rows_in[i] = q_ref[:, i * LANES : (i + 1) * LANES].astype(F32)
    lane = iota((each, LANES), 1)
    sample = iota((each, LANES), 0) % samples

    @pl.loop(0, prompts)
    def _(p):
        at = exp * prompts + p
        kept = jnp.zeros((each, LANES), jnp.int32)
        for b in range(span // KVB):
            kept = jnp.where(lane // KVB == b, live[at, blk * (span // KVB) + b], kept)
        left = jnp.minimum(lengths[at] - blk * span, span)
        prompt_ok = jnp.where(lane < left, jnp.where(kept > 0, 1, 0), 0)
        who = source[blk, at]
        held = tail_len[who, at]
        tail_ok = jnp.where(lane >= span, jnp.where(lane - span < held, 1, 0), 0)
        use = prompt_ok + jnp.where(sample == who, tail_ok, 0)
        hide = jnp.where(use > 0, 0.0, HIDE)
        hide = jnp.concatenate([hide, hide], axis=0)
        copy(p, 0).wait()
        tops = jnp.zeros((each, LANES), F32)
        sums = jnp.zeros((each, LANES), F32)
        for i in range(pairs):
            cut = slice(i * LANES, (i + 1) * LANES)
            q = jnp.concatenate(
                [rows_in[i, pl.ds(fresh * p + t, samples, stride=group), :] for t in range(fresh)],
                axis=0,
            )
            q = jnp.concatenate([jnp.where(lane < HDIM, q, 0.0), jnp.where(lane < HDIM, 0.0, q)], axis=0)
            score_buf[i] = dot(
                q.astype(BF), jnp.concatenate([k_ref[p, :, cut], tk_buf[p, :, cut]], axis=0), NT
            ) + hide
        for i in range(pairs):
            scores = score_buf[i]
            top = jnp.maximum(jnp.max(scores, axis=1, keepdims=True), FLOOR)
            top = top.astype(BF).astype(F32)
            weight = jnp.exp(scores - top)
            total = jnp.sum(weight, axis=1, keepdims=True)
            weight_buf[i] = weight.astype(BF)
            for h in range(2):
                part = slice(h * each, (h + 1) * each)
                tops = jnp.where(lane == 2 * i + h, top[part], tops)
                sums = jnp.where(lane == heads + 2 * i + h, total[part], sums)
        copy(p, 1).wait()
        copy(p, 2).wait()
        for i in range(pairs):
            cut = slice(i * LANES, (i + 1) * LANES)
            val = jnp.concatenate([v_buf[p, :, cut], tv_buf[p, :, cut]], axis=0)
            both = dot(weight_buf[i], val)
            mixed = jnp.where(lane < HDIM, both[:each], both[each:])
            for t in range(fresh):
                rows_out[i, pl.ds(fresh * p + t, samples, stride=group), :] = mixed[
                    t * samples : (t + 1) * samples
                ]
        high = sums.astype(BF).astype(F32)
        stats = tops + high + pltpu.roll(sums - high, heads, 1)
        for t in range(fresh):
            stats_in[pl.ds(fresh * p + t, samples, stride=group), :] = stats[
                t * samples : (t + 1) * samples
            ]

    for i in range(pairs):
        out_ref[:, i * LANES : (i + 1) * LANES] = rows_out[i].astype(BF)
    out_ref[:, model:] = stats_in[...].astype(BF)


def attend(lengths, live, tail_len, source, everyone, key, tail_key, value, tail_value):
    rows, model = everyone.shape
    prompts, span, _ = key.shape
    pairs = model // LANES
    cache = pltpu.VMEM((prompts, span, model), BF)
    where = pl.BlockSpec(memory_space=pl.ANY)
    return pl.pallas_call(
        attend_kernel,
        out_shape=jax.ShapeDtypeStruct((rows, model + LANES), BF),
        in_specs=[smem()] * 4 + [vmem()] * 2 + [where] * 3,
        out_specs=vmem(),
        scratch_shapes=[
            cache,
            cache,
            cache,
            pltpu.VMEM((pairs, rows, LANES), F32),
            pltpu.VMEM((pairs, rows, LANES), F32),
            pltpu.VMEM((rows, LANES), F32),
            pltpu.VMEM((pairs, 2 * rows // prompts, LANES), F32),
            pltpu.VMEM((pairs, 2 * rows // prompts, LANES), BF),
            pltpu.SemaphoreType.DMA((prompts, 3)),
        ],
        compiler_params=pltpu.CompilerParams(vmem_limit_bytes=ROOM),
        name="attend",
    )(lengths, live, tail_len, source, everyone, key, tail_key, value, tail_value)


def row_of(expert, core):
    away = jnp.where(expert % 2 == core, 0, CAP)
    return expert // 2 * (2 * CAP) + away


def combine_kernel(
    routes, got_ref, q_ref, k_ref, v_ref, h_ref, router_ref, gain_ref,
    mixed_ref, rows_ref, gate_ref, q8, k0, k1, v0, v1, spread,
):
    parts, tokens, wide = got_ref.shape
    model = wide - LANES
    heads = model // HDIM
    prompts, fresh = q_ref.shape[1], q_ref.shape[2]
    experts = router_ref.shape[0]
    for p in range(prompts):
        at = slice(fresh * p, fresh * (p + 1))
        q8[at, :] = q_ref[0, p].astype(F32)
        mixed_ref[at, :] = h_ref[0, p].astype(F32)
        key, val = k_ref[0, p].astype(F32), v_ref[0, p].astype(F32)
        k0[at, :] = jnp.broadcast_to(key[0:1], (fresh, model))
        k1[at, :] = jnp.broadcast_to(key[1:2], (fresh, model))
        v0[at, :] = jnp.broadcast_to(val[0:1], (fresh, model))
        v1[at, :] = jnp.broadcast_to(val[1:2], (fresh, model))
    spread[...] = jnp.where(
        iota((LANES, model), 1) // HDIM == iota((LANES, model), 0), 1.0, 0.0
    ).astype(BF)
    product = jnp.concatenate([q8[...] * k0[...], q8[...] * k1[...]], axis=0)
    high = product.astype(BF)
    low = (product - high.astype(F32)).astype(BF)
    own = (dot(high, spread[...], NT) + dot(low, spread[...], NT)) * 0.125
    lane = iota((tokens, LANES), 1)
    sub = iota((tokens, LANES), 0)
    s0 = own[:tokens]
    s1 = jnp.where(sub % fresh == 1, own[tokens:], HIDE)
    top = jnp.maximum(s0, s1)
    tops, sums = [], []
    for j in range(parts):
        stat = got_ref[j, :, model:].astype(F32)
        tops.append(jnp.where(lane < heads, stat, 0.0))
        total = pltpu.roll(stat, LANES - heads, 1) + pltpu.roll(stat, LANES - 2 * heads, 1)
        sums.append(jnp.where(lane < heads, total, 1.0))
        top = jnp.maximum(top, tops[-1])
    w0, w1 = jnp.exp(s0 - top), jnp.exp(s1 - top)
    scale = [jnp.exp(t - top) for t in tops]
    total = w0 + w1
    for c, l in zip(scale, sums):
        total = total + c * l
    inverse = 1.0 / total
    share = jnp.concatenate([c * inverse for c in scale] + [w0 * inverse, w1 * inverse], axis=0)
    share_high = share.astype(BF)
    share_low = (share - share_high.astype(F32)).astype(BF)
    square = jnp.zeros((tokens, LANES), F32)
    chunk = 2 * LANES
    for c in range(model // chunk):
        cut = slice(c * chunk, (c + 1) * chunk)
        each = dot(share_high, spread[:, cut]) + dot(share_low, spread[:, cut])
        here = mixed_ref[:, cut]
        for j in range(parts):
            here = here + each[j * tokens : (j + 1) * tokens] * got_ref[j, :, cut].astype(F32)
        here = here + each[parts * tokens : (parts + 1) * tokens] * v0[:, cut]
        here = here + each[(parts + 1) * tokens :] * v1[:, cut]
        mixed_ref[:, cut] = here
        for i in range(chunk // LANES):
            part = here[:, i * LANES : (i + 1) * LANES]
            square = square + part * part
    mean = jnp.sum(square, axis=1, keepdims=True) / model
    scale = lax.rsqrt(mean + 1e-05)
    normed = jnp.concatenate(
        [
            mixed_ref[:, i * LANES : (i + 1) * LANES] * scale * gain_ref[i : i + 1, :]
            for i in range(model // LANES)
        ],
        axis=1,
    )
    normed = normed.astype(BF).astype(F32)
    logits = [jnp.sum(normed * router_ref[e : e + 1, :], axis=1, keepdims=True) for e in range(experts)]
    token = iota((tokens, 1), 0)
    first = jnp.zeros((tokens, 1), jnp.int32)
    second = jnp.zeros((tokens, 1), jnp.int32)
    slots = experts * CAP
    core = lax.axis_index("expert") % 2
    row = iota((slots, tokens), 0)
    column = iota((slots, tokens), 1)
    pick = jnp.zeros((slots, tokens), F32)
    seen = jnp.zeros((slots, tokens), jnp.int32)
    for i in range(tokens):
        pair = [routes[i % fresh, r, i // fresh] for r in range(TOP)]
        first = jnp.where(token == i, pair[0], first)
        second = jnp.where(token == i, pair[1], second)
        for expert in pair:
            match = row // CAP * CAP == row_of(expert, core)
            hit = jnp.where(match, jnp.where(column == i, jnp.where(row % CAP == seen, 1.0, 0.0), 0.0), 0.0)
            pick = pick + hit
            seen = seen + jnp.where(match, 1, 0)
    logit0 = jnp.zeros((tokens, 1), F32)
    logit1 = jnp.zeros((tokens, 1), F32)
    for e in range(experts):
        logit0 = jnp.where(first == e, logits[e], logit0)
        logit1 = jnp.where(second == e, logits[e], logit1)
    gate0 = 1.0 / (1.0 + jnp.exp(logit1 - logit0))
    gate1 = 1.0 / (1.0 + jnp.exp(logit0 - logit1))
    gate_ref[...] = jnp.where(lane == 0, gate0, jnp.where(lane == 1, gate1, 0.0))
    rows_ref[...] = dot(pick, normed).astype(BF)


def combine(routes, got, query, new_key, new_value, hidden, router, gain):
    parts, tokens, wide = got.shape
    model = wide - LANES
    experts = router.shape[0]
    return pl.pallas_call(
        combine_kernel,
        out_shape=(
            jax.ShapeDtypeStruct((tokens, model), F32),
            jax.ShapeDtypeStruct((experts * CAP, model), BF),
            jax.ShapeDtypeStruct((tokens, LANES), F32),
        ),
        in_specs=[smem()] + [vmem()] * 7,
        out_specs=(vmem(), vmem(), vmem()),
        scratch_shapes=[pltpu.VMEM((tokens, model), F32)] * 5 + [pltpu.VMEM((LANES, model), BF)],
        compiler_params=pltpu.CompilerParams(vmem_limit_bytes=16 << 20),
        name="combine",
    )(routes, got, query, new_key, new_value, hidden, router, gain)


def ffn_kernel(x_ref, gate_ref, up_ref, down_ref, out_ref):
    x = x_ref[...]
    gated = dot(x, gate_ref[...], NT)
    upward = dot(x, up_ref[...], NT)
    activation = (gated / (1.0 + jnp.exp(-gated)) * upward).astype(BF)
    out_ref[...] = dot(activation, down_ref[...]).astype(BF)


def ffn(x, w_gate, w_up, w_down):
    return pl.pallas_call(
        ffn_kernel,
        out_shape=jax.ShapeDtypeStruct(x.shape, BF),
        in_specs=[vmem()] * 4,
        out_specs=vmem(),
        compiler_params=pltpu.CompilerParams(vmem_limit_bytes=16 << 20),
        cost_estimate=pl.CostEstimate(
            flops=6 * x.size * w_gate.shape[0],
            bytes_accessed=2 * (2 * x.size + 3 * w_gate.size),
            transcendentals=x.shape[0] * w_gate.shape[0],
        ),
        name="ffn",
    )(x, w_gate, w_up, w_down)


def finish_kernel(routes, mine_ref, back_ref, mixed_ref, gate_ref, weight_ref, out_ref, score_ref):
    slots, model = mine_ref.shape
    tokens = mixed_ref.shape[0]
    prompts, fresh = out_ref.shape[1], out_ref.shape[2]
    near = iota((slots, model), 0) % (2 * CAP) < CAP
    every = jnp.where(near, mine_ref[...].astype(F32), back_ref[...].astype(F32))
    core = lax.axis_index("expert") % 2
    row = iota((tokens, slots), 0)
    column = iota((tokens, slots), 1)
    seen = jnp.zeros((tokens, slots), jnp.int32)
    picks = [jnp.zeros((tokens, slots), F32) for _ in range(TOP)]
    for i in range(tokens):
        for r in range(TOP):
            match = column // CAP * CAP == row_of(routes[i % fresh, r, i // fresh], core)
            hit = jnp.where(match, jnp.where(row == i, jnp.where(column % CAP == seen, 1.0, 0.0), 0.0), 0.0)
            picks[r] = picks[r] + hit
            seen = seen + jnp.where(match, 1, 0)
    total = mixed_ref[...]
    for r in range(TOP):
        total = total + gate_ref[:, r : r + 1] * dot(picks[r], every)
    done = total.astype(BF)
    kept = done.astype(F32)
    partial = jnp.zeros((tokens, LANES), F32)
    for i in range(model // LANES):
        partial = partial + kept[:, i * LANES : (i + 1) * LANES] * weight_ref[i : i + 1, :]
    score = jnp.sum(partial, axis=1, keepdims=True)
    token = iota((tokens, LANES), 0)
    score = jnp.where(token // fresh == iota((tokens, LANES), 1), score, 0.0)
    for t in range(fresh):
        line = jnp.sum(jnp.where(token % fresh == t, score, 0.0), axis=0, keepdims=True)
        score_ref[t : t + 1, :] = line[:, :prompts]
    for p in range(prompts):
        out_ref[0, p] = done[fresh * p : fresh * (p + 1)]


def finish(routes, mine, back, mixed, gates, weight):
    tokens, model = mixed.shape
    fresh, _, prompts = routes.shape
    return pl.pallas_call(
        finish_kernel,
        out_shape=(
            jax.ShapeDtypeStruct((1, prompts, fresh, model), BF),
            jax.ShapeDtypeStruct((fresh, prompts), F32),
        ),
        in_specs=[smem()] + [vmem()] * 5,
        out_specs=(vmem(), vmem()),
        compiler_params=pltpu.CompilerParams(vmem_limit_bytes=16 << 20),
        name="finish",
    )(routes, mine, back, mixed, gates, weight)


def exchange(x, axis):
    return lax.all_to_all(x, axis, 0, 0, tiled=True)


def local(
    hidden,
    query,
    new_key,
    new_value,
    prompt_key,
    prompt_value,
    prompt_len,
    live_blocks,
    tail_key,
    tail_value,
    tail_len,
    tail_source,
    routes,
    router,
    ffn_gain,
    w_gate,
    w_up,
    w_down,
    score_weight,
):
    blk_count = lax.axis_size("blk")
    prompts, fresh, model = query.shape[1:]
    tokens = prompts * fresh
    everyone = exchange(share(query, blk_count), "blk")
    chosen = routes[0].transpose(1, 2, 0)
    sent = attend(
        prompt_len,
        live_blocks,
        tail_len,
        tail_source,
        everyone.reshape(blk_count * tokens, model),
        prompt_key,
        tail_key[0],
        prompt_value,
        tail_value[0],
    )
    got = exchange(sent.reshape(blk_count, tokens, -1), "blk")
    mixed, outgoing, gates = combine(
        chosen, got, query, new_key, new_value, hidden, router.T, ffn_gain.reshape(-1, LANES)
    )
    exp_count = lax.axis_size("expert")
    both = ("blk", "expert")
    side = 4
    planes = exp_count // 2
    device = lambda x, z, y, c: (x * side + z) * exp_count + y * 2 + c
    swap = [(i, i ^ 1) for i in range(exp_count)]
    lines = [
        [device(o, k, y, 1) if c == 0 else device(k, o, y, 0) for k in range(side) for y in range(planes)]
        for c in range(2)
        for o in range(side)
    ]

    def shift(step):
        moves = []
        for x in range(side):
            for z in range(side):
                for y in range(planes):
                    moves.append((device(x, z, y, 1), device((x + step) % side, z, y, 1)))
                    moves.append((device(x, z, y, 0), device(x, (z + step) % side, y, 0)))
        return moves

    wide = (planes, 2 * CAP, model)
    near = jnp.arange(2 * CAP)[None, :, None] < CAP
    rows = jnp.where(
        near, outgoing.reshape(wide), lax.ppermute(outgoing, "expert", swap).reshape(wide)
    )
    rows = jnp.broadcast_to(rows[None], (side, *wide)).reshape(-1, 2 * CAP, model)
    rows = lax.all_to_all(rows, both, 0, 0, tiled=True, axis_index_groups=lines)
    rows = rows.reshape(-1, model)
    weights = (w_gate[0].T, w_up[0].T, w_down[0])
    order = (2, 1, 3)
    arrivals = [lax.ppermute(rows, both, shift(s)) for s in order]
    total = ffn(rows, *weights)
    parts = [total]
    for s, arrived in zip(order, arrivals):
        arrived, parts[0] = lax.optimization_barrier((arrived, parts[0]))
        parts.append(lax.ppermute(ffn(arrived, *weights), both, shift(-s)))
    total = sum(part.astype(F32) for part in parts).astype(BF)
    total = lax.all_to_all(
        total.reshape(-1, 2 * CAP, model), both, 0, 0, tiled=True, axis_index_groups=lines
    )
    total = total.reshape(side, -1, model)
    mine = jnp.sum(total.astype(F32), axis=0).astype(BF)
    back = lax.ppermute(mine, "expert", swap)
    layer_out, score = finish(chosen, mine, back, mixed, gates, score_weight.reshape(-1, LANES))
    return layer_out, score.T[None]


def solution(mesh):
    token = P("blk", "expert", None, None)
    cache = P("expert", "blk", None)
    columns = P("expert", None, "blk")
    placed = (
        token, token, token, token, cache, cache, P(), P(), token, token, P(), P(), token, P(), P(),
        columns, columns, cache, P(),
    )
    return jax.shard_map(
        local,
        mesh=mesh,
        in_specs=placed,
        out_specs=(token, P("blk", "expert", None)),
        check_vma=False,
    )
```

```python
import jax
import jax.numpy as jnp
from jax import lax
from jax.experimental import pallas as pl
from jax.experimental.pallas import tpu as pltpu
from jax.sharding import PartitionSpec as P

HDIM = 64
TOP = 2
KVB = 16
CAP = 4
LANES = 128
ROOM = 51 << 20

BF = jnp.bfloat16
F32 = jnp.float32
HIDE = -1e30
FLOOR = -1e4
NT = (((1,), (1,)), ((), ()))


def vmem():
    return pl.BlockSpec(memory_space=pltpu.VMEM)


def smem():
    return pl.BlockSpec(memory_space=pltpu.SMEM)


def iota(shape, dim):
    return lax.broadcasted_iota(jnp.int32, shape, dim)


def dot(a, b, dims=(((1,), (0,)), ((), ()))):
    return lax.dot_general(a, b, dims, preferred_element_type=F32)


def share_kernel(q_ref, out_ref, flat):
    prompts, fresh = q_ref.shape[1], q_ref.shape[2]
    for p in range(prompts):
        flat[fresh * p : fresh * (p + 1), :] = q_ref[0, p].astype(F32) * 0.125
    rows = flat[...].astype(BF)
    for m in range(out_ref.shape[0]):
        out_ref[m] = rows


def share(query, samples):
    _, prompts, fresh, model = query.shape
    tokens = prompts * fresh
    return pl.pallas_call(
        share_kernel,
        out_shape=jax.ShapeDtypeStruct((samples, tokens, model), BF),
        in_specs=[vmem()],
        out_specs=vmem(),
        scratch_shapes=[pltpu.VMEM((tokens, model), F32)],
        compiler_params=pltpu.CompilerParams(vmem_limit_bytes=16 << 20),
        name="share",
    )(query)


def attend_kernel(
    lengths, live, tail_len, source, q_ref, k_ref, tk_hbm, v_hbm, tv_hbm, out_ref,
    tk_buf, v_buf, tv_buf, rows_in, rows_out, stats_in, score_buf, weight_buf, sems,
):
    prompts, span, model = k_ref.shape
    rows = q_ref.shape[0]
    fresh = 2
    group = prompts * fresh
    samples = rows // group
    each = fresh * samples
    heads = model // HDIM
    pairs = model // LANES
    blk, exp = lax.axis_index("blk"), lax.axis_index("expert")
    moves = ((tk_hbm, tk_buf), (v_hbm, v_buf), (tv_hbm, tv_buf))

    def copy(p, i):
        src, dst = moves[i]
        return pltpu.make_async_copy(src.at[p], dst.at[p], sems.at[p, i])

    for p in range(prompts):
        for i in range(len(moves)):
            copy(p, i).start()
    for i in range(pairs):
        rows_in[i] = q_ref[:, i * LANES : (i + 1) * LANES].astype(F32)
    lane = iota((each, LANES), 1)
    sample = iota((each, LANES), 0) % samples

    @pl.loop(0, prompts)
    def _(p):
        at = exp * prompts + p
        kept = jnp.zeros((each, LANES), jnp.int32)
        for b in range(span // KVB):
            kept = jnp.where(lane // KVB == b, live[at, blk * (span // KVB) + b], kept)
        left = jnp.minimum(lengths[at] - blk * span, span)
        prompt_ok = jnp.where(lane < left, jnp.where(kept > 0, 1, 0), 0)
        who = source[blk, at]
        held = tail_len[who, at]
        tail_ok = jnp.where(lane >= span, jnp.where(lane - span < held, 1, 0), 0)
        use = prompt_ok + jnp.where(sample == who, tail_ok, 0)
        hide = jnp.where(use > 0, 0.0, HIDE)
        hide = jnp.concatenate([hide, hide], axis=0)
        copy(p, 0).wait()
        tops = jnp.zeros((each, LANES), F32)
        sums = jnp.zeros((each, LANES), F32)
        for i in range(pairs):
            cut = slice(i * LANES, (i + 1) * LANES)
            q = jnp.concatenate(
                [rows_in[i, pl.ds(fresh * p + t, samples, stride=group), :] for t in range(fresh)],
                axis=0,
            )
            q = jnp.concatenate([jnp.where(lane < HDIM, q, 0.0), jnp.where(lane < HDIM, 0.0, q)], axis=0)
            score_buf[i] = dot(
                q.astype(BF), jnp.concatenate([k_ref[p, :, cut], tk_buf[p, :, cut]], axis=0), NT
            ) + hide
        for i in range(pairs):
            scores = score_buf[i]
            top = jnp.maximum(jnp.max(scores, axis=1, keepdims=True), FLOOR)
            top = top.astype(BF).astype(F32)
            weight = jnp.exp(scores - top)
            total = jnp.sum(weight, axis=1, keepdims=True)
            weight_buf[i] = weight.astype(BF)
            for h in range(2):
                part = slice(h * each, (h + 1) * each)
                tops = jnp.where(lane == 2 * i + h, top[part], tops)
                sums = jnp.where(lane == heads + 2 * i + h, total[part], sums)
        copy(p, 1).wait()
        copy(p, 2).wait()
        for i in range(pairs):
            cut = slice(i * LANES, (i + 1) * LANES)
            val = jnp.concatenate([v_buf[p, :, cut], tv_buf[p, :, cut]], axis=0)
            both = dot(weight_buf[i], val)
            mixed = jnp.where(lane < HDIM, both[:each], both[each:])
            for t in range(fresh):
                rows_out[i, pl.ds(fresh * p + t, samples, stride=group), :] = mixed[
                    t * samples : (t + 1) * samples
                ]
        high = sums.astype(BF).astype(F32)
        stats = tops + high + pltpu.roll(sums - high, heads, 1)
        for t in range(fresh):
            stats_in[pl.ds(fresh * p + t, samples, stride=group), :] = stats[
                t * samples : (t + 1) * samples
            ]

    for i in range(pairs):
        out_ref[:, i * LANES : (i + 1) * LANES] = rows_out[i].astype(BF)
    out_ref[:, model:] = stats_in[...].astype(BF)


def attend(lengths, live, tail_len, source, everyone, key, tail_key, value, tail_value):
    rows, model = everyone.shape
    prompts, span, _ = key.shape
    pairs = model // LANES
    cache = pltpu.VMEM((prompts, span, model), BF)
    where = pl.BlockSpec(memory_space=pl.ANY)
    return pl.pallas_call(
        attend_kernel,
        out_shape=jax.ShapeDtypeStruct((rows, model + LANES), BF),
        in_specs=[smem()] * 4 + [vmem()] * 2 + [where] * 3,
        out_specs=vmem(),
        scratch_shapes=[
            cache,
            cache,
            cache,
            pltpu.VMEM((pairs, rows, LANES), F32),
            pltpu.VMEM((pairs, rows, LANES), F32),
            pltpu.VMEM((rows, LANES), F32),
            pltpu.VMEM((pairs, 2 * rows // prompts, LANES), F32),
            pltpu.VMEM((pairs, 2 * rows // prompts, LANES), BF),
            pltpu.SemaphoreType.DMA((prompts, 3)),
        ],
        compiler_params=pltpu.CompilerParams(vmem_limit_bytes=ROOM),
        name="attend",
    )(lengths, live, tail_len, source, everyone, key, tail_key, value, tail_value)


def row_of(expert, core):
    away = jnp.where(expert % 2 == core, 0, CAP)
    return expert // 2 * (2 * CAP) + away


def combine_kernel(
    routes, got_ref, q_ref, k_ref, v_ref, h_ref, router_ref, gain_ref,
    mixed_ref, rows_ref, gate_ref, q8, k0, k1, v0, v1, spread,
):
    parts, tokens, wide = got_ref.shape
    model = wide - LANES
    heads = model // HDIM
    prompts, fresh = q_ref.shape[1], q_ref.shape[2]
    experts = router_ref.shape[0]
    for p in range(prompts):
        at = slice(fresh * p, fresh * (p + 1))
        q8[at, :] = q_ref[0, p].astype(F32)
        mixed_ref[at, :] = h_ref[0, p].astype(F32)
        key, val = k_ref[0, p].astype(F32), v_ref[0, p].astype(F32)
        k0[at, :] = jnp.broadcast_to(key[0:1], (fresh, model))
        k1[at, :] = jnp.broadcast_to(key[1:2], (fresh, model))
        v0[at, :] = jnp.broadcast_to(val[0:1], (fresh, model))
        v1[at, :] = jnp.broadcast_to(val[1:2], (fresh, model))
    spread[...] = jnp.where(
        iota((LANES, model), 1) // HDIM == iota((LANES, model), 0), 1.0, 0.0
    ).astype(BF)
    product = jnp.concatenate([q8[...] * k0[...], q8[...] * k1[...]], axis=0)
    high = product.astype(BF)
    low = (product - high.astype(F32)).astype(BF)
    own = (dot(high, spread[...], NT) + dot(low, spread[...], NT)) * 0.125
    lane = iota((tokens, LANES), 1)
    sub = iota((tokens, LANES), 0)
    s0 = own[:tokens]
    s1 = jnp.where(sub % fresh == 1, own[tokens:], HIDE)
    top = jnp.maximum(s0, s1)
    tops, sums = [], []
    for j in range(parts):
        stat = got_ref[j, :, model:].astype(F32)
        tops.append(jnp.where(lane < heads, stat, 0.0))
        total = pltpu.roll(stat, LANES - heads, 1) + pltpu.roll(stat, LANES - 2 * heads, 1)
        sums.append(jnp.where(lane < heads, total, 1.0))
        top = jnp.maximum(top, tops[-1])
    w0, w1 = jnp.exp(s0 - top), jnp.exp(s1 - top)
    scale = [jnp.exp(t - top) for t in tops]
    total = w0 + w1
    for c, l in zip(scale, sums):
        total = total + c * l
    inverse = 1.0 / total
    share = jnp.concatenate([c * inverse for c in scale] + [w0 * inverse, w1 * inverse], axis=0)
    share_high = share.astype(BF)
    share_low = (share - share_high.astype(F32)).astype(BF)
    square = jnp.zeros((tokens, LANES), F32)
    chunk = 2 * LANES
    for c in range(model // chunk):
        cut = slice(c * chunk, (c + 1) * chunk)
        each = dot(share_high, spread[:, cut]) + dot(share_low, spread[:, cut])
        here = mixed_ref[:, cut]
        for j in range(parts):
            here = here + each[j * tokens : (j + 1) * tokens] * got_ref[j, :, cut].astype(F32)
        here = here + each[parts * tokens : (parts + 1) * tokens] * v0[:, cut]
        here = here + each[(parts + 1) * tokens :] * v1[:, cut]
        mixed_ref[:, cut] = here
        for i in range(chunk // LANES):
            part = here[:, i * LANES : (i + 1) * LANES]
            square = square + part * part
    mean = jnp.sum(square, axis=1, keepdims=True) / model
    scale = lax.rsqrt(mean + 1e-05)
    normed = jnp.concatenate(
        [
            mixed_ref[:, i * LANES : (i + 1) * LANES] * scale * gain_ref[i : i + 1, :]
            for i in range(model // LANES)
        ],
        axis=1,
    )
    normed = normed.astype(BF).astype(F32)
    logits = [jnp.sum(normed * router_ref[e : e + 1, :], axis=1, keepdims=True) for e in range(experts)]
    token = iota((tokens, 1), 0)
    first = jnp.zeros((tokens, 1), jnp.int32)
    second = jnp.zeros((tokens, 1), jnp.int32)
    slots = experts * CAP
    core = lax.axis_index("expert") % 2
    row = iota((slots, tokens), 0)
    column = iota((slots, tokens), 1)
    pick = jnp.zeros((slots, tokens), F32)
    seen = jnp.zeros((slots, tokens), jnp.int32)
    for i in range(tokens):
        pair = [routes[i % fresh, r, i // fresh] for r in range(TOP)]
        first = jnp.where(token == i, pair[0], first)
        second = jnp.where(token == i, pair[1], second)
        for expert in pair:
            match = row // CAP * CAP == row_of(expert, core)
            hit = jnp.where(match, jnp.where(column == i, jnp.where(row % CAP == seen, 1.0, 0.0), 0.0), 0.0)
            pick = pick + hit
            seen = seen + jnp.where(match, 1, 0)
    logit0 = jnp.zeros((tokens, 1), F32)
    logit1 = jnp.zeros((tokens, 1), F32)
    for e in range(experts):
        logit0 = jnp.where(first == e, logits[e], logit0)
        logit1 = jnp.where(second == e, logits[e], logit1)
    gate0 = 1.0 / (1.0 + jnp.exp(logit1 - logit0))
    gate1 = 1.0 / (1.0 + jnp.exp(logit0 - logit1))
    gate_ref[...] = jnp.where(lane == 0, gate0, jnp.where(lane == 1, gate1, 0.0))
    rows_ref[...] = dot(pick, normed).astype(BF)


def combine(routes, got, query, new_key, new_value, hidden, router, gain):
    parts, tokens, wide = got.shape
    model = wide - LANES
    experts = router.shape[0]
    return pl.pallas_call(
        combine_kernel,
        out_shape=(
            jax.ShapeDtypeStruct((tokens, model), F32),
            jax.ShapeDtypeStruct((experts * CAP, model), BF),
            jax.ShapeDtypeStruct((tokens, LANES), F32),
        ),
        in_specs=[smem()] + [vmem()] * 7,
        out_specs=(vmem(), vmem(), vmem()),
        scratch_shapes=[pltpu.VMEM((tokens, model), F32)] * 5 + [pltpu.VMEM((LANES, model), BF)],
        compiler_params=pltpu.CompilerParams(vmem_limit_bytes=16 << 20),
        name="combine",
    )(routes, got, query, new_key, new_value, hidden, router, gain)


def ffn(xs, weights):
    count = len(xs)
    rows, model = xs[0].shape
    units = weights[2].shape[0]

    def kernel(*refs):
        gate_ref, up_ref, down_ref = refs[count : count + 3]
        x = jnp.concatenate([ref[...] for ref in refs[:count]], axis=0)
        gated = dot(x, gate_ref[...], NT)
        upward = dot(x, up_ref[...], NT)
        activation = (gated / (1.0 + jnp.exp(-gated)) * upward).astype(BF)
        result = dot(activation, down_ref[...]).astype(BF)
        for i in range(count):
            refs[count + 3 + i][...] = result[i * rows : (i + 1) * rows]

    return pl.pallas_call(
        kernel,
        out_shape=(jax.ShapeDtypeStruct((rows, model), BF),) * count,
        in_specs=[vmem()] * (count + 3),
        out_specs=(vmem(),) * count,
        compiler_params=pltpu.CompilerParams(vmem_limit_bytes=16 << 20),
        cost_estimate=pl.CostEstimate(
            flops=6 * count * rows * model * units,
            bytes_accessed=4 * count * rows * model + 6 * units * model,
            transcendentals=count * rows * units,
        ),
        name="ffn",
    )(*xs, *weights)


def finish_kernel(routes, mine_ref, back_ref, mixed_ref, gate_ref, weight_ref, out_ref, score_ref):
    slots, model = mine_ref.shape
    tokens = mixed_ref.shape[0]
    prompts, fresh = out_ref.shape[1], out_ref.shape[2]
    near = iota((slots, model), 0) % (2 * CAP) < CAP
    every = jnp.where(near, mine_ref[...].astype(F32), back_ref[...].astype(F32))
    core = lax.axis_index("expert") % 2
    row = iota((tokens, slots), 0)
    column = iota((tokens, slots), 1)
    seen = jnp.zeros((tokens, slots), jnp.int32)
    picks = [jnp.zeros((tokens, slots), F32) for _ in range(TOP)]
    for i in range(tokens):
        for r in range(TOP):
            match = column // CAP * CAP == row_of(routes[i % fresh, r, i // fresh], core)
            hit = jnp.where(match, jnp.where(row == i, jnp.where(column % CAP == seen, 1.0, 0.0), 0.0), 0.0)
            picks[r] = picks[r] + hit
            seen = seen + jnp.where(match, 1, 0)
    total = mixed_ref[...]
    for r in range(TOP):
        total = total + gate_ref[:, r : r + 1] * dot(picks[r], every)
    done = total.astype(BF)
    kept = done.astype(F32)
    partial = jnp.zeros((tokens, LANES), F32)
    for i in range(model // LANES):
        partial = partial + kept[:, i * LANES : (i + 1) * LANES] * weight_ref[i : i + 1, :]
    score = jnp.sum(partial, axis=1, keepdims=True)
    token = iota((tokens, LANES), 0)
    score = jnp.where(token // fresh == iota((tokens, LANES), 1), score, 0.0)
    for t in range(fresh):
        line = jnp.sum(jnp.where(token % fresh == t, score, 0.0), axis=0, keepdims=True)
        score_ref[t : t + 1, :] = line[:, :prompts]
    for p in range(prompts):
        out_ref[0, p] = done[fresh * p : fresh * (p + 1)]


def finish(routes, mine, back, mixed, gates, weight):
    tokens, model = mixed.shape
    fresh, _, prompts = routes.shape
    return pl.pallas_call(
        finish_kernel,
        out_shape=(
            jax.ShapeDtypeStruct((1, prompts, fresh, model), BF),
            jax.ShapeDtypeStruct((fresh, prompts), F32),
        ),
        in_specs=[smem()] + [vmem()] * 5,
        out_specs=(vmem(), vmem()),
        compiler_params=pltpu.CompilerParams(vmem_limit_bytes=16 << 20),
        name="finish",
    )(routes, mine, back, mixed, gates, weight)


def exchange(x, axis):
    return lax.all_to_all(x, axis, 0, 0, tiled=True)


def local(
    hidden,
    query,
    new_key,
    new_value,
    prompt_key,
    prompt_value,
    prompt_len,
    live_blocks,
    tail_key,
    tail_value,
    tail_len,
    tail_source,
    routes,
    router,
    ffn_gain,
    w_gate,
    w_up,
    w_down,
    score_weight,
):
    blk_count = lax.axis_size("blk")
    prompts, fresh, model = query.shape[1:]
    tokens = prompts * fresh
    everyone = exchange(share(query, blk_count), "blk")
    chosen = routes[0].transpose(1, 2, 0)
    sent = attend(
        prompt_len,
        live_blocks,
        tail_len,
        tail_source,
        everyone.reshape(blk_count * tokens, model),
        prompt_key,
        tail_key[0],
        prompt_value,
        tail_value[0],
    )
    got = exchange(sent.reshape(blk_count, tokens, -1), "blk")
    mixed, outgoing, gates = combine(
        chosen, got, query, new_key, new_value, hidden, router.T, ffn_gain.reshape(-1, LANES)
    )
    exp_count = lax.axis_size("expert")
    both = ("blk", "expert")
    side = 4
    planes = exp_count // 2
    device = lambda x, z, y, c: (x * side + z) * exp_count + y * 2 + c
    swap = [(i, i ^ 1) for i in range(exp_count)]
    lines = [
        [device(o, k, y, 1) if c == 0 else device(k, o, y, 0) for k in range(side) for y in range(planes)]
        for c in range(2)
        for o in range(side)
    ]

    def shift(step):
        moves = []
        for x in range(side):
            for z in range(side):
                for y in range(planes):
                    moves.append((device(x, z, y, 1), device((x + step) % side, z, y, 1)))
                    moves.append((device(x, z, y, 0), device(x, (z + step) % side, y, 0)))
        return moves

    wide = (planes, 2 * CAP, model)
    near = jnp.arange(2 * CAP)[None, :, None] < CAP
    rows = jnp.where(
        near, outgoing.reshape(wide), lax.ppermute(outgoing, "expert", swap).reshape(wide)
    )
    rows = jnp.broadcast_to(rows[None], (side, *wide)).reshape(-1, 2 * CAP, model)
    rows = lax.all_to_all(rows, both, 0, 0, tiled=True, axis_index_groups=lines)
    rows = rows.reshape(-1, model)
    weights = (w_gate[0].T, w_up[0].T, w_down[0])
    send = lambda x, step: lax.ppermute(x, both, shift(step))
    far, before, after = send(rows, 2), send(rows, 1), send(rows, 3)
    (own,) = ffn((rows,), weights)
    far, own = lax.optimization_barrier((far, own))
    (far,) = ffn((far,), weights)
    home = send(far, -2)
    before, after, _ = lax.optimization_barrier((before, after, far))
    before, after = ffn((before, after), weights)
    after, before = send(after, -3), send(before, -1)
    partial = own.astype(F32) + home.astype(F32)
    partial, after, before = lax.optimization_barrier((partial, after, before))
    total = (partial + after.astype(F32) + before.astype(F32)).astype(BF)
    total = lax.all_to_all(
        total.reshape(-1, 2 * CAP, model), both, 0, 0, tiled=True, axis_index_groups=lines
    )
    total = total.reshape(side, -1, model)
    mine = jnp.sum(total.astype(F32), axis=0).astype(BF)
    back = lax.ppermute(mine, "expert", swap)
    layer_out, score = finish(chosen, mine, back, mixed, gates, score_weight.reshape(-1, LANES))
    return layer_out, score.T[None]


def solution(mesh):
    token = P("blk", "expert", None, None)
    cache = P("expert", "blk", None)
    columns = P("expert", None, "blk")
    placed = (
        token, token, token, token, cache, cache, P(), P(), token, token, P(), P(), token, P(), P(),
        columns, columns, cache, P(),
    )
    return jax.shard_map(
        local,
        mesh=mesh,
        in_specs=placed,
        out_specs=(token, P("blk", "expert", None)),
        check_vma=False,
    )
```

```python
import jax
import jax.numpy as jnp
from jax import lax
from jax.experimental import pallas as pl
from jax.experimental.pallas import tpu as pltpu
from jax.sharding import PartitionSpec as P

HDIM = 64
TOP = 2
KVB = 16
CAP = 4
LANES = 128
ROOM = 51 << 20

BF = jnp.bfloat16
F32 = jnp.float32
HIDE = -1e30
FLOOR = -1e4
NT = (((1,), (1,)), ((), ()))


def vmem():
    return pl.BlockSpec(memory_space=pltpu.VMEM)


def smem():
    return pl.BlockSpec(memory_space=pltpu.SMEM)


def iota(shape, dim):
    return lax.broadcasted_iota(jnp.int32, shape, dim)


def dot(a, b, dims=(((1,), (0,)), ((), ()))):
    return lax.dot_general(a, b, dims, preferred_element_type=F32)


def share_kernel(q_ref, out_ref, flat):
    prompts, fresh = q_ref.shape[1], q_ref.shape[2]
    for p in range(prompts):
        flat[fresh * p : fresh * (p + 1), :] = q_ref[0, p].astype(F32) * 0.125
    rows = flat[...].astype(BF)
    for m in range(out_ref.shape[0]):
        out_ref[m] = rows


def share(query, samples):
    _, prompts, fresh, model = query.shape
    tokens = prompts * fresh
    return pl.pallas_call(
        share_kernel,
        out_shape=jax.ShapeDtypeStruct((samples, tokens, model), BF),
        in_specs=[vmem()],
        out_specs=vmem(),
        scratch_shapes=[pltpu.VMEM((tokens, model), F32)],
        compiler_params=pltpu.CompilerParams(vmem_limit_bytes=16 << 20),
        name="share",
    )(query)


def attend_kernel(
    lengths, live, tail_len, source, q_ref, k_ref, fresh_ref, tk_hbm, v_hbm, tv_hbm, out_ref, own_ref,
    tk_buf, v_buf, tv_buf, rows_in, rows_out, stats_in, score_buf, weight_buf, sems,
):
    prompts, span, model = k_ref.shape
    rows = q_ref.shape[0]
    fresh = 2
    group = prompts * fresh
    samples = rows // group
    each = fresh * samples
    heads = model // HDIM
    pairs = model // LANES
    blk, exp = lax.axis_index("blk"), lax.axis_index("expert")
    moves = ((tk_hbm, tk_buf), (v_hbm, v_buf), (tv_hbm, tv_buf))

    def copy(p, i):
        src, dst = moves[i]
        return pltpu.make_async_copy(src.at[p], dst.at[p], sems.at[p, i])

    for p in range(prompts):
        for i in range(len(moves)):
            copy(p, i).start()
    for i in range(pairs):
        rows_in[i] = q_ref[:, i * LANES : (i + 1) * LANES].astype(F32)
    own = pl.ds(pl.multiple_of(blk * group, group), group)
    even = iota((group, LANES), 0) % fresh == 0
    columns = iota((group, LANES), 1)
    for u in range(fresh):
        own_ref[u] = jnp.zeros((group, LANES), F32)
    for i in range(pairs):
        cut = slice(i * LANES, (i + 1) * LANES)
        mine = rows_in[i, own, :]
        for u in range(fresh):
            key = jnp.concatenate(
                [
                    jnp.broadcast_to(fresh_ref[0, p, u : u + 1, cut].astype(F32), (fresh, LANES))
                    for p in range(prompts)
                ],
                axis=0,
            )
            product = mine * key
            low = jnp.sum(jnp.where(columns < HDIM, product, 0.0), axis=1, keepdims=True)
            high = jnp.sum(jnp.where(columns < HDIM, 0.0, product), axis=1, keepdims=True)
            score = jnp.where(columns == 2 * i, low, jnp.where(columns == 2 * i + 1, high, own_ref[u]))
            own_ref[u] = jnp.where(even, HIDE, score) if u == 1 else score
    lane = iota((each, LANES), 1)
    sample = iota((each, LANES), 0) % samples

    @pl.loop(0, prompts)
    def _(p):
        at = exp * prompts + p
        kept = jnp.zeros((each, LANES), jnp.int32)
        for b in range(span // KVB):
            kept = jnp.where(lane // KVB == b, live[at, blk * (span // KVB) + b], kept)
        left = jnp.minimum(lengths[at] - blk * span, span)
        prompt_ok = jnp.where(lane < left, jnp.where(kept > 0, 1, 0), 0)
        who = source[blk, at]
        held = tail_len[who, at]
        tail_ok = jnp.where(lane >= span, jnp.where(lane - span < held, 1, 0), 0)
        use = prompt_ok + jnp.where(sample == who, tail_ok, 0)
        hide = jnp.where(use > 0, 0.0, HIDE)
        hide = jnp.concatenate([hide, hide], axis=0)
        copy(p, 0).wait()
        tops = jnp.zeros((each, LANES), F32)
        sums = jnp.zeros((each, LANES), F32)
        for i in range(pairs):
            cut = slice(i * LANES, (i + 1) * LANES)
            q = jnp.concatenate(
                [rows_in[i, pl.ds(fresh * p + t, samples, stride=group), :] for t in range(fresh)],
                axis=0,
            )
            q = jnp.concatenate([jnp.where(lane < HDIM, q, 0.0), jnp.where(lane < HDIM, 0.0, q)], axis=0)
            score_buf[i] = dot(
                q.astype(BF), jnp.concatenate([k_ref[p, :, cut], tk_buf[p, :, cut]], axis=0), NT
            ) + hide
        for i in range(pairs):
            scores = score_buf[i]
            top = jnp.maximum(jnp.max(scores, axis=1, keepdims=True), FLOOR)
            top = top.astype(BF).astype(F32)
            weight = jnp.exp(scores - top)
            total = jnp.sum(weight, axis=1, keepdims=True)
            weight_buf[i] = weight.astype(BF)
            for h in range(2):
                part = slice(h * each, (h + 1) * each)
                tops = jnp.where(lane == 2 * i + h, top[part], tops)
                sums = jnp.where(lane == heads + 2 * i + h, total[part], sums)
        copy(p, 1).wait()
        copy(p, 2).wait()
        for i in range(pairs):
            cut = slice(i * LANES, (i + 1) * LANES)
            val = jnp.concatenate([v_buf[p, :, cut], tv_buf[p, :, cut]], axis=0)
            both = dot(weight_buf[i], val)
            mixed = jnp.where(lane < HDIM, both[:each], both[each:])
            for t in range(fresh):
                rows_out[i, pl.ds(fresh * p + t, samples, stride=group), :] = mixed[
                    t * samples : (t + 1) * samples
                ]
        high = sums.astype(BF).astype(F32)
        stats = tops + high + pltpu.roll(sums - high, heads, 1)
        for t in range(fresh):
            stats_in[pl.ds(fresh * p + t, samples, stride=group), :] = stats[
                t * samples : (t + 1) * samples
            ]

    for i in range(pairs):
        out_ref[:, i * LANES : (i + 1) * LANES] = rows_out[i].astype(BF)
    out_ref[:, model:] = stats_in[...].astype(BF)


def attend(lengths, live, tail_len, source, everyone, key, new_key, tail_key, value, tail_value):
    rows, model = everyone.shape
    prompts, span, _ = key.shape
    pairs = model // LANES
    cache = pltpu.VMEM((prompts, span, model), BF)
    where = pl.BlockSpec(memory_space=pl.ANY)
    return pl.pallas_call(
        attend_kernel,
        out_shape=(
            jax.ShapeDtypeStruct((rows, model + LANES), BF),
            jax.ShapeDtypeStruct((new_key.shape[2], new_key.shape[1] * new_key.shape[2], LANES), F32),
        ),
        in_specs=[smem()] * 4 + [vmem()] * 3 + [where] * 3,
        out_specs=(vmem(), vmem()),
        scratch_shapes=[
            cache,
            cache,
            cache,
            pltpu.VMEM((pairs, rows, LANES), F32),
            pltpu.VMEM((pairs, rows, LANES), F32),
            pltpu.VMEM((rows, LANES), F32),
            pltpu.VMEM((pairs, 2 * rows // prompts, LANES), F32),
            pltpu.VMEM((pairs, 2 * rows // prompts, LANES), BF),
            pltpu.SemaphoreType.DMA((prompts, 3)),
        ],
        compiler_params=pltpu.CompilerParams(vmem_limit_bytes=ROOM),
        name="attend",
    )(lengths, live, tail_len, source, everyone, key, new_key, tail_key, value, tail_value)


def row_of(expert, core):
    away = jnp.where(expert % 2 == core, 0, CAP)
    return expert // 2 * (2 * CAP) + away


def combine_kernel(
    routes, got_ref, own_ref, v_ref, h_ref, router_ref, gain_ref,
    mixed_ref, rows_ref, gate_ref, v0, v1, spread,
):
    parts, tokens, wide = got_ref.shape
    model = wide - LANES
    heads = model // HDIM
    prompts, fresh = v_ref.shape[1], v_ref.shape[2]
    experts = router_ref.shape[0]
    for p in range(prompts):
        at = slice(fresh * p, fresh * (p + 1))
        mixed_ref[at, :] = h_ref[0, p].astype(F32)
        val = v_ref[0, p].astype(F32)
        v0[at, :] = jnp.broadcast_to(val[0:1], (fresh, model))
        v1[at, :] = jnp.broadcast_to(val[1:2], (fresh, model))
    spread[...] = jnp.where(
        iota((LANES, model), 1) // HDIM == iota((LANES, model), 0), 1.0, 0.0
    ).astype(BF)
    lane = iota((tokens, LANES), 1)
    s0, s1 = own_ref[0], own_ref[1]
    top = jnp.maximum(s0, s1)
    tops, sums = [], []
    for j in range(parts):
        stat = got_ref[j, :, model:].astype(F32)
        tops.append(jnp.where(lane < heads, stat, 0.0))
        total = pltpu.roll(stat, LANES - heads, 1) + pltpu.roll(stat, LANES - 2 * heads, 1)
        sums.append(jnp.where(lane < heads, total, 1.0))
        top = jnp.maximum(top, tops[-1])
    w0, w1 = jnp.exp(s0 - top), jnp.exp(s1 - top)
    scale = [jnp.exp(t - top) for t in tops]
    total = w0 + w1
    for c, l in zip(scale, sums):
        total = total + c * l
    inverse = 1.0 / total
    share = jnp.concatenate([c * inverse for c in scale] + [w0 * inverse, w1 * inverse], axis=0)
    share_high = share.astype(BF)
    share_low = (share - share_high.astype(F32)).astype(BF)
    square = jnp.zeros((tokens, LANES), F32)
    chunk = 2 * LANES
    for c in range(model // chunk):
        cut = slice(c * chunk, (c + 1) * chunk)
        each = dot(share_high, spread[:, cut]) + dot(share_low, spread[:, cut])
        here = mixed_ref[:, cut]
        for j in range(parts):
            here = here + each[j * tokens : (j + 1) * tokens] * got_ref[j, :, cut].astype(F32)
        here = here + each[parts * tokens : (parts + 1) * tokens] * v0[:, cut]
        here = here + each[(parts + 1) * tokens :] * v1[:, cut]
        mixed_ref[:, cut] = here
        for i in range(chunk // LANES):
            part = here[:, i * LANES : (i + 1) * LANES]
            square = square + part * part
    mean = jnp.sum(square, axis=1, keepdims=True) / model
    scale = lax.rsqrt(mean + 1e-05)
    normed = jnp.concatenate(
        [
            mixed_ref[:, i * LANES : (i + 1) * LANES] * scale * gain_ref[i : i + 1, :]
            for i in range(model // LANES)
        ],
        axis=1,
    )
    normed = normed.astype(BF).astype(F32)
    logits = [jnp.sum(normed * router_ref[e : e + 1, :], axis=1, keepdims=True) for e in range(experts)]
    token = iota((tokens, 1), 0)
    first = jnp.zeros((tokens, 1), jnp.int32)
    second = jnp.zeros((tokens, 1), jnp.int32)
    slots = experts * CAP
    core = lax.axis_index("expert") % 2
    row = iota((slots, tokens), 0)
    column = iota((slots, tokens), 1)
    pick = jnp.zeros((slots, tokens), F32)
    seen = jnp.zeros((slots, tokens), jnp.int32)
    for i in range(tokens):
        pair = [routes[i % fresh, r, i // fresh] for r in range(TOP)]
        first = jnp.where(token == i, pair[0], first)
        second = jnp.where(token == i, pair[1], second)
        for expert in pair:
            match = row // CAP * CAP == row_of(expert, core)
            hit = jnp.where(match, jnp.where(column == i, jnp.where(row % CAP == seen, 1.0, 0.0), 0.0), 0.0)
            pick = pick + hit
            seen = seen + jnp.where(match, 1, 0)
    logit0 = jnp.zeros((tokens, 1), F32)
    logit1 = jnp.zeros((tokens, 1), F32)
    for e in range(experts):
        logit0 = jnp.where(first == e, logits[e], logit0)
        logit1 = jnp.where(second == e, logits[e], logit1)
    gate0 = 1.0 / (1.0 + jnp.exp(logit1 - logit0))
    gate1 = 1.0 / (1.0 + jnp.exp(logit0 - logit1))
    gate_ref[...] = jnp.where(lane == 0, gate0, jnp.where(lane == 1, gate1, 0.0))
    rows_ref[...] = dot(pick, normed).astype(BF)


def combine(routes, got, own, new_value, hidden, router, gain):
    parts, tokens, wide = got.shape
    model = wide - LANES
    experts = router.shape[0]
    return pl.pallas_call(
        combine_kernel,
        out_shape=(
            jax.ShapeDtypeStruct((tokens, model), F32),
            jax.ShapeDtypeStruct((experts * CAP, model), BF),
            jax.ShapeDtypeStruct((tokens, LANES), F32),
        ),
        in_specs=[smem()] + [vmem()] * 6,
        out_specs=(vmem(), vmem(), vmem()),
        scratch_shapes=[pltpu.VMEM((tokens, model), F32)] * 2 + [pltpu.VMEM((LANES, model), BF)],
        compiler_params=pltpu.CompilerParams(vmem_limit_bytes=16 << 20),
        name="combine",
    )(routes, got, own, new_value, hidden, router, gain)


def ffn(xs, weights):
    count = len(xs)
    rows, model = xs[0].shape
    units = weights[2].shape[0]

    def kernel(*refs):
        gate_ref, up_ref, down_ref = refs[count : count + 3]
        x = jnp.concatenate([ref[...] for ref in refs[:count]], axis=0)
        gated = dot(x, gate_ref[...], NT)
        upward = dot(x, up_ref[...], NT)
        activation = (gated / (1.0 + jnp.exp(-gated)) * upward).astype(BF)
        result = dot(activation, down_ref[...]).astype(BF)
        for i in range(count):
            refs[count + 3 + i][...] = result[i * rows : (i + 1) * rows]

    return pl.pallas_call(
        kernel,
        out_shape=(jax.ShapeDtypeStruct((rows, model), BF),) * count,
        in_specs=[vmem()] * (count + 3),
        out_specs=(vmem(),) * count,
        compiler_params=pltpu.CompilerParams(vmem_limit_bytes=16 << 20),
        cost_estimate=pl.CostEstimate(
            flops=6 * count * rows * model * units,
            bytes_accessed=4 * count * rows * model + 6 * units * model,
            transcendentals=count * rows * units,
        ),
        name="ffn",
    )(*xs, *weights)


def finish_kernel(routes, mine_ref, back_ref, mixed_ref, gate_ref, weight_ref, out_ref, score_ref):
    slots, model = mine_ref.shape
    tokens = mixed_ref.shape[0]
    prompts, fresh = out_ref.shape[1], out_ref.shape[2]
    near = iota((slots, model), 0) % (2 * CAP) < CAP
    every = jnp.where(near, mine_ref[...].astype(F32), back_ref[...].astype(F32))
    core = lax.axis_index("expert") % 2
    row = iota((tokens, slots), 0)
    column = iota((tokens, slots), 1)
    seen = jnp.zeros((tokens, slots), jnp.int32)
    picks = [jnp.zeros((tokens, slots), F32) for _ in range(TOP)]
    for i in range(tokens):
        for r in range(TOP):
            match = column // CAP * CAP == row_of(routes[i % fresh, r, i // fresh], core)
            hit = jnp.where(match, jnp.where(row == i, jnp.where(column % CAP == seen, 1.0, 0.0), 0.0), 0.0)
            picks[r] = picks[r] + hit
            seen = seen + jnp.where(match, 1, 0)
    total = mixed_ref[...]
    for r in range(TOP):
        total = total + gate_ref[:, r : r + 1] * dot(picks[r], every)
    done = total.astype(BF)
    kept = done.astype(F32)
    partial = jnp.zeros((tokens, LANES), F32)
    for i in range(model // LANES):
        partial = partial + kept[:, i * LANES : (i + 1) * LANES] * weight_ref[i : i + 1, :]
    score = jnp.sum(partial, axis=1, keepdims=True)
    token = iota((tokens, LANES), 0)
    score = jnp.where(token // fresh == iota((tokens, LANES), 1), score, 0.0)
    for t in range(fresh):
        line = jnp.sum(jnp.where(token % fresh == t, score, 0.0), axis=0, keepdims=True)
        score_ref[t : t + 1, :] = line[:, :prompts]
    for p in range(prompts):
        out_ref[0, p] = done[fresh * p : fresh * (p + 1)]


def finish(routes, mine, back, mixed, gates, weight):
    tokens, model = mixed.shape
    fresh, _, prompts = routes.shape
    return pl.pallas_call(
        finish_kernel,
        out_shape=(
            jax.ShapeDtypeStruct((1, prompts, fresh, model), BF),
            jax.ShapeDtypeStruct((fresh, prompts), F32),
        ),
        in_specs=[smem()] + [vmem()] * 5,
        out_specs=(vmem(), vmem()),
        compiler_params=pltpu.CompilerParams(vmem_limit_bytes=16 << 20),
        name="finish",
    )(routes, mine, back, mixed, gates, weight)


def exchange(x, axis):
    return lax.all_to_all(x, axis, 0, 0, tiled=True)


def local(
    hidden,
    query,
    new_key,
    new_value,
    prompt_key,
    prompt_value,
    prompt_len,
    live_blocks,
    tail_key,
    tail_value,
    tail_len,
    tail_source,
    routes,
    router,
    ffn_gain,
    w_gate,
    w_up,
    w_down,
    score_weight,
):
    blk_count = lax.axis_size("blk")
    prompts, fresh, model = query.shape[1:]
    tokens = prompts * fresh
    everyone = exchange(share(query, blk_count), "blk")
    chosen = routes[0].transpose(1, 2, 0)
    sent, own_scores = attend(
        prompt_len,
        live_blocks,
        tail_len,
        tail_source,
        everyone.reshape(blk_count * tokens, model),
        prompt_key,
        new_key,
        tail_key[0],
        prompt_value,
        tail_value[0],
    )
    got = exchange(sent.reshape(blk_count, tokens, -1), "blk")
    mixed, outgoing, gates = combine(
        chosen, got, own_scores, new_value, hidden, router.T, ffn_gain.reshape(-1, LANES)
    )
    exp_count = lax.axis_size("expert")
    both = ("blk", "expert")
    side = 4
    planes = exp_count // 2
    device = lambda x, z, y, c: (x * side + z) * exp_count + y * 2 + c
    swap = [(i, i ^ 1) for i in range(exp_count)]
    lines = [
        [device(o, k, y, 1) if c == 0 else device(k, o, y, 0) for k in range(side) for y in range(planes)]
        for c in range(2)
        for o in range(side)
    ]

    def shift(step):
        moves = []
        for x in range(side):
            for z in range(side):
                for y in range(planes):
                    moves.append((device(x, z, y, 1), device((x + step) % side, z, y, 1)))
                    moves.append((device(x, z, y, 0), device(x, (z + step) % side, y, 0)))
        return moves

    wide = (planes, 2 * CAP, model)
    near = jnp.arange(2 * CAP)[None, :, None] < CAP
    rows = jnp.where(
        near, outgoing.reshape(wide), lax.ppermute(outgoing, "expert", swap).reshape(wide)
    )
    rows = jnp.broadcast_to(rows[None], (side, *wide)).reshape(-1, 2 * CAP, model)
    rows = lax.all_to_all(rows, both, 0, 0, tiled=True, axis_index_groups=lines)
    rows = rows.reshape(-1, model)
    weights = (w_gate[0].T, w_up[0].T, w_down[0])
    send = lambda x, step: lax.ppermute(x, both, shift(step))
    far, before, after = send(rows, 2), send(rows, 1), send(rows, 3)
    (own,) = ffn((rows,), weights)
    far, own = lax.optimization_barrier((far, own))
    (far,) = ffn((far,), weights)
    home = send(far, -2)
    before, after, _ = lax.optimization_barrier((before, after, far))
    before, after = ffn((before, after), weights)
    after, before = send(after, -3), send(before, -1)
    partial = own.astype(F32) + home.astype(F32)
    partial, after, before = lax.optimization_barrier((partial, after, before))
    total = (partial + after.astype(F32) + before.astype(F32)).astype(BF)
    total = lax.all_to_all(
        total.reshape(-1, 2 * CAP, model), both, 0, 0, tiled=True, axis_index_groups=lines
    )
    total = total.reshape(side, -1, model)
    mine = jnp.sum(total.astype(F32), axis=0).astype(BF)
    back = lax.ppermute(mine, "expert", swap)
    layer_out, score = finish(chosen, mine, back, mixed, gates, score_weight.reshape(-1, LANES))
    return layer_out, score.T[None]


def solution(mesh):
    token = P("blk", "expert", None, None)
    cache = P("expert", "blk", None)
    columns = P("expert", None, "blk")
    placed = (
        token, token, token, token, cache, cache, P(), P(), token, token, P(), P(), token, P(), P(),
        columns, columns, cache, P(),
    )
    return jax.shard_map(
        local,
        mesh=mesh,
        in_specs=placed,
        out_specs=(token, P("blk", "expert", None)),
        check_vma=False,
    )
```

```python
import jax
import jax.numpy as jnp
from jax import lax
from jax.experimental import pallas as pl
from jax.experimental.pallas import tpu as pltpu
from jax.sharding import PartitionSpec as P

HDIM = 64
TOP = 2
KVB = 16
CAP = 4
LANES = 128
ROOM = 51 << 20

BF = jnp.bfloat16
F32 = jnp.float32
HIDE = -1e30
FLOOR = -1e4
NT = (((1,), (1,)), ((), ()))


def vmem():
    return pl.BlockSpec(memory_space=pltpu.VMEM)


def smem():
    return pl.BlockSpec(memory_space=pltpu.SMEM)


def iota(shape, dim):
    return lax.broadcasted_iota(jnp.int32, shape, dim)


def dot(a, b, dims=(((1,), (0,)), ((), ()))):
    return lax.dot_general(a, b, dims, preferred_element_type=F32)


def share_kernel(q_ref, out_ref, flat):
    prompts, fresh = q_ref.shape[1], q_ref.shape[2]
    for p in range(prompts):
        flat[fresh * p : fresh * (p + 1), :] = q_ref[0, p].astype(F32) * 0.125
    rows = flat[...].astype(BF)
    for m in range(out_ref.shape[0]):
        out_ref[m] = rows


def share(query, samples):
    _, prompts, fresh, model = query.shape
    tokens = prompts * fresh
    return pl.pallas_call(
        share_kernel,
        out_shape=jax.ShapeDtypeStruct((samples, tokens, model), BF),
        in_specs=[vmem()],
        out_specs=vmem(),
        scratch_shapes=[pltpu.VMEM((tokens, model), F32)],
        compiler_params=pltpu.CompilerParams(vmem_limit_bytes=16 << 20),
        name="share",
    )(query)


def attend_kernel(
    lengths, live, tail_len, source, q_ref, k_ref, fresh_ref, tk_hbm, v_hbm, tv_hbm, out_ref, own_ref,
    tk_buf, v_buf, tv_buf, rows_in, rows_out, stats_in, score_buf, weight_buf, sems,
):
    prompts, span, model = k_ref.shape
    rows = q_ref.shape[0]
    fresh = 2
    group = prompts * fresh
    samples = rows // group
    each = fresh * samples
    heads = model // HDIM
    pairs = model // LANES
    blk, exp = lax.axis_index("blk"), lax.axis_index("expert")
    moves = ((tk_hbm, tk_buf), (v_hbm, v_buf), (tv_hbm, tv_buf))

    def copy(p, i):
        src, dst = moves[i]
        return pltpu.make_async_copy(src.at[p], dst.at[p], sems.at[p, i])

    for p in range(prompts):
        for i in range(len(moves)):
            copy(p, i).start()
    for i in range(pairs):
        rows_in[i] = q_ref[:, i * LANES : (i + 1) * LANES].astype(F32)
    own = pl.ds(pl.multiple_of(blk * group, group), group)
    even = iota((group, LANES), 0) % fresh == 0
    columns = iota((group, LANES), 1)
    for u in range(fresh):
        own_ref[u] = jnp.zeros((group, LANES), F32)
    for i in range(pairs):
        cut = slice(i * LANES, (i + 1) * LANES)
        mine = rows_in[i, own, :]
        for u in range(fresh):
            key = jnp.concatenate(
                [
                    jnp.broadcast_to(fresh_ref[0, p, u : u + 1, cut].astype(F32), (fresh, LANES))
                    for p in range(prompts)
                ],
                axis=0,
            )
            product = mine * key
            low = jnp.sum(jnp.where(columns < HDIM, product, 0.0), axis=1, keepdims=True)
            high = jnp.sum(jnp.where(columns < HDIM, 0.0, product), axis=1, keepdims=True)
            score = jnp.where(columns == 2 * i, low, jnp.where(columns == 2 * i + 1, high, own_ref[u]))
            own_ref[u] = jnp.where(even, HIDE, score) if u == 1 else score
    lane = iota((each, LANES), 1)
    sample = iota((each, LANES), 0) % samples

    @pl.loop(0, prompts)
    def _(p):
        at = exp * prompts + p
        kept = jnp.zeros((each, LANES), jnp.int32)
        for b in range(span // KVB):
            kept = jnp.where(lane // KVB == b, live[at, blk * (span // KVB) + b], kept)
        left = jnp.minimum(lengths[at] - blk * span, span)
        prompt_ok = jnp.where(lane < left, jnp.where(kept > 0, 1, 0), 0)
        who = source[blk, at]
        held = tail_len[who, at]
        tail_ok = jnp.where(lane >= span, jnp.where(lane - span < held, 1, 0), 0)
        use = prompt_ok + jnp.where(sample == who, tail_ok, 0)
        hide = jnp.where(use > 0, 0.0, HIDE)
        hide = jnp.concatenate([hide, hide], axis=0)
        copy(p, 0).wait()
        tops = jnp.zeros((each, LANES), F32)
        sums = jnp.zeros((each, LANES), F32)
        for i in range(pairs):
            cut = slice(i * LANES, (i + 1) * LANES)
            q = jnp.concatenate(
                [rows_in[i, pl.ds(fresh * p + t, samples, stride=group), :] for t in range(fresh)],
                axis=0,
            )
            q = jnp.concatenate([jnp.where(lane < HDIM, q, 0.0), jnp.where(lane < HDIM, 0.0, q)], axis=0)
            score_buf[i] = dot(
                q.astype(BF), jnp.concatenate([k_ref[p, :, cut], tk_buf[p, :, cut]], axis=0), NT
            ) + hide
        for i in range(pairs):
            scores = score_buf[i]
            top = jnp.maximum(jnp.max(scores, axis=1, keepdims=True), FLOOR)
            top = top.astype(BF).astype(F32)
            weight = jnp.exp(scores - top)
            total = jnp.sum(weight, axis=1, keepdims=True)
            weight_buf[i] = weight.astype(BF)
            for h in range(2):
                part = slice(h * each, (h + 1) * each)
                tops = jnp.where(lane == 2 * i + h, top[part], tops)
                sums = jnp.where(lane == heads + 2 * i + h, total[part], sums)
        copy(p, 1).wait()
        copy(p, 2).wait()
        for i in range(pairs):
            cut = slice(i * LANES, (i + 1) * LANES)
            val = jnp.concatenate([v_buf[p, :, cut], tv_buf[p, :, cut]], axis=0)
            both = dot(weight_buf[i], val)
            mixed = jnp.where(lane < HDIM, both[:each], both[each:])
            for t in range(fresh):
                rows_out[i, pl.ds(fresh * p + t, samples, stride=group), :] = mixed[
                    t * samples : (t + 1) * samples
                ]
        high = sums.astype(BF).astype(F32)
        stats = tops + high + pltpu.roll(sums - high, heads, 1)
        for t in range(fresh):
            stats_in[pl.ds(fresh * p + t, samples, stride=group), :] = stats[
                t * samples : (t + 1) * samples
            ]

    for i in range(pairs):
        out_ref[:, i * LANES : (i + 1) * LANES] = rows_out[i].astype(BF)
    out_ref[:, model:] = stats_in[...].astype(BF)


def attend(lengths, live, tail_len, source, everyone, key, new_key, tail_key, value, tail_value):
    rows, model = everyone.shape
    prompts, span, _ = key.shape
    pairs = model // LANES
    cache = pltpu.VMEM((prompts, span, model), BF)
    where = pl.BlockSpec(memory_space=pl.ANY)
    return pl.pallas_call(
        attend_kernel,
        out_shape=(
            jax.ShapeDtypeStruct((rows, model + LANES), BF),
            jax.ShapeDtypeStruct((new_key.shape[2], new_key.shape[1] * new_key.shape[2], LANES), F32),
        ),
        in_specs=[smem()] * 4 + [vmem()] * 3 + [where] * 3,
        out_specs=(vmem(), vmem()),
        scratch_shapes=[
            cache,
            cache,
            cache,
            pltpu.VMEM((pairs, rows, LANES), F32),
            pltpu.VMEM((pairs, rows, LANES), F32),
            pltpu.VMEM((rows, LANES), F32),
            pltpu.VMEM((pairs, 2 * rows // prompts, LANES), F32),
            pltpu.VMEM((pairs, 2 * rows // prompts, LANES), BF),
            pltpu.SemaphoreType.DMA((prompts, 3)),
        ],
        compiler_params=pltpu.CompilerParams(vmem_limit_bytes=ROOM),
        name="attend",
    )(lengths, live, tail_len, source, everyone, key, new_key, tail_key, value, tail_value)


def row_of(expert, core):
    away = jnp.where(expert % 2 == core, 0, CAP)
    return expert // 2 * (2 * CAP) + away


def combine_kernel(
    routes, got_ref, own_ref, v_ref, h_ref, router_ref, gain_ref,
    mixed_ref, rows_ref, gate_ref, v0, v1, spread,
):
    parts, tokens, wide = got_ref.shape
    model = wide - LANES
    heads = model // HDIM
    prompts, fresh = v_ref.shape[1], v_ref.shape[2]
    experts = router_ref.shape[0]
    for p in range(prompts):
        at = slice(fresh * p, fresh * (p + 1))
        mixed_ref[at, :] = h_ref[0, p].astype(F32)
        val = v_ref[0, p].astype(F32)
        v0[at, :] = jnp.broadcast_to(val[0:1], (fresh, model))
        v1[at, :] = jnp.broadcast_to(val[1:2], (fresh, model))
    spread[...] = jnp.where(
        iota((LANES, model), 1) // HDIM == iota((LANES, model), 0), 1.0, 0.0
    ).astype(BF)
    lane = iota((tokens, LANES), 1)
    s0, s1 = own_ref[0], own_ref[1]
    top = jnp.maximum(s0, s1)
    tops, sums = [], []
    for j in range(parts):
        stat = got_ref[j, :, model:].astype(F32)
        tops.append(jnp.where(lane < heads, stat, 0.0))
        total = pltpu.roll(stat, LANES - heads, 1) + pltpu.roll(stat, LANES - 2 * heads, 1)
        sums.append(jnp.where(lane < heads, total, 1.0))
        top = jnp.maximum(top, tops[-1])
    w0, w1 = jnp.exp(s0 - top), jnp.exp(s1 - top)
    scale = [jnp.exp(t - top) for t in tops]
    total = w0 + w1
    for c, l in zip(scale, sums):
        total = total + c * l
    inverse = 1.0 / total
    share = jnp.concatenate([c * inverse for c in scale] + [w0 * inverse, w1 * inverse], axis=0)
    share_high = share.astype(BF)
    share_low = (share - share_high.astype(F32)).astype(BF)
    square = jnp.zeros((tokens, LANES), F32)
    chunk = 2 * LANES
    for c in range(model // chunk):
        cut = slice(c * chunk, (c + 1) * chunk)
        each = dot(share_high, spread[:, cut]) + dot(share_low, spread[:, cut])
        here = mixed_ref[:, cut]
        for j in range(parts):
            here = here + each[j * tokens : (j + 1) * tokens] * got_ref[j, :, cut].astype(F32)
        here = here + each[parts * tokens : (parts + 1) * tokens] * v0[:, cut]
        here = here + each[(parts + 1) * tokens :] * v1[:, cut]
        mixed_ref[:, cut] = here
        for i in range(chunk // LANES):
            part = here[:, i * LANES : (i + 1) * LANES]
            square = square + part * part
    mean = jnp.sum(square, axis=1, keepdims=True) / model
    scale = lax.rsqrt(mean + 1e-05)
    normed = jnp.concatenate(
        [
            mixed_ref[:, i * LANES : (i + 1) * LANES] * scale * gain_ref[i : i + 1, :]
            for i in range(model // LANES)
        ],
        axis=1,
    )
    normed = normed.astype(BF).astype(F32)
    logits = [jnp.sum(normed * router_ref[e : e + 1, :], axis=1, keepdims=True) for e in range(experts)]
    token = iota((tokens, 1), 0)
    first = jnp.zeros((tokens, 1), jnp.int32)
    second = jnp.zeros((tokens, 1), jnp.int32)
    slots = experts * CAP
    core = lax.axis_index("expert") % 2
    row = iota((slots, tokens), 0)
    column = iota((slots, tokens), 1)
    pick = jnp.zeros((slots, tokens), F32)
    seen = jnp.zeros((slots, tokens), jnp.int32)
    for i in range(tokens):
        pair = [routes[i % fresh, r, i // fresh] for r in range(TOP)]
        first = jnp.where(token == i, pair[0], first)
        second = jnp.where(token == i, pair[1], second)
        for expert in pair:
            match = row // CAP * CAP == row_of(expert, core)
            hit = jnp.where(match, jnp.where(column == i, jnp.where(row % CAP == seen, 1.0, 0.0), 0.0), 0.0)
            pick = pick + hit
            seen = seen + jnp.where(match, 1, 0)
    logit0 = jnp.zeros((tokens, 1), F32)
    logit1 = jnp.zeros((tokens, 1), F32)
    for e in range(experts):
        logit0 = jnp.where(first == e, logits[e], logit0)
        logit1 = jnp.where(second == e, logits[e], logit1)
    gate0 = 1.0 / (1.0 + jnp.exp(logit1 - logit0))
    gate1 = 1.0 / (1.0 + jnp.exp(logit0 - logit1))
    gate_ref[...] = jnp.where(lane == 0, gate0, jnp.where(lane == 1, gate1, 0.0))
    rows_ref[...] = dot(pick, normed).astype(BF)


def combine(routes, got, own, new_value, hidden, router, gain):
    parts, tokens, wide = got.shape
    model = wide - LANES
    experts = router.shape[0]
    return pl.pallas_call(
        combine_kernel,
        out_shape=(
            jax.ShapeDtypeStruct((tokens, model), F32),
            jax.ShapeDtypeStruct((experts * CAP, model), BF),
            jax.ShapeDtypeStruct((tokens, LANES), F32),
        ),
        in_specs=[smem()] + [vmem()] * 6,
        out_specs=(vmem(), vmem(), vmem()),
        scratch_shapes=[pltpu.VMEM((tokens, model), F32)] * 2 + [pltpu.VMEM((LANES, model), BF)],
        compiler_params=pltpu.CompilerParams(vmem_limit_bytes=16 << 20),
        name="combine",
    )(routes, got, own, new_value, hidden, router, gain)


def ffn(xs, weights):
    count = len(xs)
    rows, model = xs[0].shape
    units = weights[2].shape[0]

    def kernel(*refs):
        gate_ref, up_ref, down_ref = refs[count : count + 3]
        x = jnp.concatenate([ref[...] for ref in refs[:count]], axis=0)
        gated = dot(x, gate_ref[...], NT)
        upward = dot(x, up_ref[...], NT)
        activation = (gated / (1.0 + jnp.exp(-gated)) * upward).astype(BF)
        result = dot(activation, down_ref[...]).astype(BF)
        for i in range(count):
            refs[count + 3 + i][...] = result[i * rows : (i + 1) * rows]

    return pl.pallas_call(
        kernel,
        out_shape=(jax.ShapeDtypeStruct((rows, model), BF),) * count,
        in_specs=[vmem()] * (count + 3),
        out_specs=(vmem(),) * count,
        compiler_params=pltpu.CompilerParams(vmem_limit_bytes=16 << 20),
        cost_estimate=pl.CostEstimate(
            flops=6 * count * rows * model * units,
            bytes_accessed=4 * count * rows * model + 6 * units * model,
            transcendentals=count * rows * units,
        ),
        name="ffn",
    )(*xs, *weights)


def finish_kernel(routes, mine_ref, back_ref, mixed_ref, gate_ref, weight_ref, out_ref, score_ref):
    slots, model = mine_ref.shape
    tokens = mixed_ref.shape[0]
    prompts, fresh = out_ref.shape[1], out_ref.shape[2]
    near = iota((slots, model), 0) % (2 * CAP) < CAP
    every = jnp.where(near, mine_ref[...].astype(F32), back_ref[...].astype(F32))
    core = lax.axis_index("expert") % 2
    row = iota((tokens, slots), 0)
    column = iota((tokens, slots), 1)
    seen = jnp.zeros((tokens, slots), jnp.int32)
    picks = [jnp.zeros((tokens, slots), F32) for _ in range(TOP)]
    for i in range(tokens):
        for r in range(TOP):
            match = column // CAP * CAP == row_of(routes[i % fresh, r, i // fresh], core)
            hit = jnp.where(match, jnp.where(row == i, jnp.where(column % CAP == seen, 1.0, 0.0), 0.0), 0.0)
            picks[r] = picks[r] + hit
            seen = seen + jnp.where(match, 1, 0)
    total = mixed_ref[...]
    for r in range(TOP):
        total = total + gate_ref[:, r : r + 1] * dot(picks[r], every)
    done = total.astype(BF)
    kept = done.astype(F32)
    partial = jnp.zeros((tokens, LANES), F32)
    for i in range(model // LANES):
        partial = partial + kept[:, i * LANES : (i + 1) * LANES] * weight_ref[i : i + 1, :]
    score = jnp.sum(partial, axis=1, keepdims=True)
    token = iota((tokens, LANES), 0)
    score = jnp.where(token // fresh == iota((tokens, LANES), 1), score, 0.0)
    for t in range(fresh):
        line = jnp.sum(jnp.where(token % fresh == t, score, 0.0), axis=0, keepdims=True)
        score_ref[t : t + 1, :] = line[:, :prompts]
    for p in range(prompts):
        out_ref[0, p] = done[fresh * p : fresh * (p + 1)]


def finish(routes, mine, back, mixed, gates, weight):
    tokens, model = mixed.shape
    fresh, _, prompts = routes.shape
    return pl.pallas_call(
        finish_kernel,
        out_shape=(
            jax.ShapeDtypeStruct((1, prompts, fresh, model), BF),
            jax.ShapeDtypeStruct((fresh, prompts), F32),
        ),
        in_specs=[smem()] + [vmem()] * 5,
        out_specs=(vmem(), vmem()),
        compiler_params=pltpu.CompilerParams(vmem_limit_bytes=16 << 20),
        name="finish",
    )(routes, mine, back, mixed, gates, weight)


def exchange(x, axis):
    return lax.all_to_all(x, axis, 0, 0, tiled=True)


def local(
    hidden,
    query,
    new_key,
    new_value,
    prompt_key,
    prompt_value,
    prompt_len,
    live_blocks,
    tail_key,
    tail_value,
    tail_len,
    tail_source,
    routes,
    router,
    ffn_gain,
    w_gate,
    w_up,
    w_down,
    score_weight,
):
    blk_count = lax.axis_size("blk")
    prompts, fresh, model = query.shape[1:]
    tokens = prompts * fresh
    everyone = exchange(share(query, blk_count), "blk")
    chosen = routes[0].transpose(1, 2, 0)
    sent, own_scores = attend(
        prompt_len,
        live_blocks,
        tail_len,
        tail_source,
        everyone.reshape(blk_count * tokens, model),
        prompt_key,
        new_key,
        tail_key[0],
        prompt_value,
        tail_value[0],
    )
    got = exchange(sent.reshape(blk_count, tokens, -1), "blk")
    mixed, outgoing, gates = combine(
        chosen, got, own_scores, new_value, hidden, router.T, ffn_gain.reshape(-1, LANES)
    )
    exp_count = lax.axis_size("expert")
    both = ("blk", "expert")
    side = 4
    planes = exp_count // 2
    device = lambda x, z, y, c: (x * side + z) * exp_count + y * 2 + c
    swap = [(i, i ^ 1) for i in range(exp_count)]
    lines = [
        [device(o, k, y, 1) if c == 0 else device(k, o, y, 0) for k in range(side) for y in range(planes)]
        for c in range(2)
        for o in range(side)
    ]

    def shift(step):
        moves = []
        for x in range(side):
            for z in range(side):
                for y in range(planes):
                    moves.append((device(x, z, y, 1), device((x + step) % side, z, y, 1)))
                    moves.append((device(x, z, y, 0), device(x, (z + step) % side, y, 0)))
        return moves

    wide = (planes, 2 * CAP, model)
    near = jnp.arange(2 * CAP)[None, :, None] < CAP
    rows = jnp.where(
        near, outgoing.reshape(wide), lax.ppermute(outgoing, "expert", swap).reshape(wide)
    )
    rows = jnp.broadcast_to(rows[None], (side, *wide)).reshape(-1, 2 * CAP, model)
    rows = lax.all_to_all(rows, both, 0, 0, tiled=True, axis_index_groups=lines)
    rows = rows.reshape(-1, model)
    weights = (w_gate[0].T, w_up[0].T, w_down[0])
    send = lambda x, step: lax.ppermute(x, both, shift(step))
    far, after, before = send(rows, 2), send(rows, 3), send(rows, 1)
    (own,) = ffn((rows,), weights)
    far, own = lax.optimization_barrier((far, own))
    (far,) = ffn((far,), weights)
    home = send(far, -2)
    after, before, _ = lax.optimization_barrier((after, before, far))
    after, before = ffn((after, before), weights)
    before, after = send(before, -1), send(after, -3)
    partial = own.astype(F32) + home.astype(F32)
    partial, before, after = lax.optimization_barrier((partial, before, after))
    total = (partial + before.astype(F32) + after.astype(F32)).astype(BF)
    total = lax.all_to_all(
        total.reshape(-1, 2 * CAP, model), both, 0, 0, tiled=True, axis_index_groups=lines
    )
    total = total.reshape(side, -1, model)
    mine = jnp.sum(total.astype(F32), axis=0).astype(BF)
    back = lax.ppermute(mine, "expert", swap)
    layer_out, score = finish(chosen, mine, back, mixed, gates, score_weight.reshape(-1, LANES))
    return layer_out, score.T[None]


def solution(mesh):
    token = P("blk", "expert", None, None)
    cache = P("expert", "blk", None)
    columns = P("expert", None, "blk")
    placed = (
        token, token, token, token, cache, cache, P(), P(), token, token, P(), P(), token, P(), P(),
        columns, columns, cache, P(),
    )
    return jax.shard_map(
        local,
        mesh=mesh,
        in_specs=placed,
        out_specs=(token, P("blk", "expert", None)),
        check_vma=False,
    )
```
